256 devices in a mesh: leaf: 64 (over z, y, core), off: 4 (over x).
Axes of the slice: x: 4, y: 4, z: 8, core: 2. Of those that a mesh axis runs over, the one named last changes fastest.
Arguments:
- multipoles: bfloat16 [65536, 488], P('leaf'), may hold values from -6 to 6
- kernels: bfloat16 [40, 488, 488], P('off'), may hold values from -0.0390625 to 0.0390625
- transfer: bfloat16 [8, 488, 488], replicated, may hold values from -0.09375 to 0.09375
- leaf_target: int32 [64, 40, 1024], P('leaf', 'off'), may hold values from 0 to 1023, as said below
- leaf_source: int32 [64, 40, 1024], P('leaf', 'off'), may hold values from 0 to 1407
- leaf_count: int32 [64, 40], P('leaf', 'off'), may hold values from 512 to 1024
- coarse_target: int32 [64, 40, 128], P('leaf', 'off'), may hold values from 0 to 127, as said below
- coarse_source: int32 [64, 40, 128], P('leaf', 'off'), may hold values from 0 to 223
- coarse_count: int32 [64, 40], P('leaf', 'off'), may hold values from 64 to 128
- ghost_send: int32 [64, 6, 64], P('leaf'), may hold values from 0 to 1343, as said below
- coarse_send: int32 [64, 6, 16], P('leaf'), may hold values from 0 to 207, as said below
Outputs:
- expansions: float32 [65536, 488], P(('leaf', 'off'))
The draws below stay inside these ranges and needn't reach their ends.
Inputs may be any that keep to these rules, and one draw needn't show every extreme that they name: Per partition and class, leaf_target is a permutation of 0 to 1023. Per partition and class, coarse_target is a permutation of 0 to 127. `ghost_send`: in round b every index is below 1024 + b * 64. `coarse_send`: in round b every index is below 128 + b * 16.
All inputs are finite; a program needn't handle non-finite values.
Results may differ from the reference program's by a relative error of at most 0.0009.
Values may be sent and summed in bfloat16 or wider, within the bound.
A program may use at most 64 MiB of HBM per device.

```python
import jax
import jax.numpy as jnp
from jax import lax

P_SIZE = 488
BOX_DEV = 1024
GHOST = 64
GHOST_C = 16
ROUNDS = 6
PAR_DEV = 128
BUF = 1408
CBUF = 224
CLASSES = 40
BOXES = 65536
N_LEAF = 64


def distinct_perm(key, leading, length):
    scores = jax.random.randint(key, leading + (length,), 0, 1 << 20) * length + jnp.arange(length)
    return jnp.argsort(scores, axis=-1).astype(jnp.int32)


def draw_leaf_target(key, part):
    return distinct_perm(jax.random.fold_in(key, 11), (N_LEAF, CLASSES), BOX_DEV)


def draw_coarse_target(key, part):
    return distinct_perm(jax.random.fold_in(key, 12), (N_LEAF, CLASSES), PAR_DEV)


def draw_leaf_source(key, part):
    chosen = jax.random.randint(jax.random.fold_in(key, 13), (N_LEAF, CLASSES, BOX_DEV), 0, BUF)
    return chosen.at[0, 0, 0].set(BUF - 1).at[0, 0, 1].set(0).astype(jnp.int32)


def draw_coarse_source(key, part):
    chosen = jax.random.randint(jax.random.fold_in(key, 14), (N_LEAF, CLASSES, PAR_DEV), 0, CBUF)
    return chosen.at[0, 0, 0].set(CBUF - 1).at[0, 0, 1].set(0).astype(jnp.int32)


def draw_leaf_count(key, part):
    chosen = jax.random.randint(jax.random.fold_in(key, 15), (N_LEAF, CLASSES), BOX_DEV // 2, BOX_DEV + 1)
    return chosen.at[0, 0].set(BOX_DEV).at[N_LEAF - 1, 0].set(BOX_DEV // 2).astype(jnp.int32)


def draw_coarse_count(key, part):
    chosen = jax.random.randint(jax.random.fold_in(key, 16), (N_LEAF, CLASSES), PAR_DEV // 2, PAR_DEV + 1)
    return chosen.at[0, 0].set(PAR_DEV).at[N_LEAF - 1, 0].set(PAR_DEV // 2).astype(jnp.int32)


def draw_ghost_send(key, part):
    ceiling = (BOX_DEV + jnp.arange(ROUNDS) * GHOST)[None, :, None]
    chosen = jax.random.randint(jax.random.fold_in(key, 17), (N_LEAF, ROUNDS, GHOST), 0, ceiling)
    return chosen.at[0, ROUNDS - 1, 0].set(BOX_DEV + (ROUNDS - 1) * GHOST - 1).at[0, 0, 1].set(0).astype(jnp.int32)


def draw_coarse_send(key, part):
    ceiling = (PAR_DEV + jnp.arange(ROUNDS) * GHOST_C)[None, :, None]
    chosen = jax.random.randint(jax.random.fold_in(key, 18), (N_LEAF, ROUNDS, GHOST_C), 0, ceiling)
    return chosen.at[0, ROUNDS - 1, 0].set(PAR_DEV + (ROUNDS - 1) * GHOST_C - 1).at[0, 0, 1].set(0).astype(jnp.int32)


def levels(own_key, dims, pieces, least, high):
    def one(axis_at, shards_of):
        steps = jax.random.uniform(jax.random.fold_in(jax.random.fold_in(own_key, 6), axis_at), (shards_of,), jnp.float32, least / len(pieces), high / len(pieces))
        return jnp.repeat(jnp.exp(steps), dims[axis_at] // shards_of).reshape((-1,) + (1,) * (len(dims) - axis_at - 1))

    level = one(*pieces[0])
    for cut in pieces[1:]:
        level = level * one(*cut)
    return level


def noise(stream_key, dims, scale, limit, pieces=(), kind=jnp.bfloat16):
    level = levels(stream_key, dims, pieces, -0.22, 0.18) if pieces else 1.0
    entries = jax.random.normal(stream_key, dims, jnp.float32) * scale * level
    return jnp.minimum(jnp.maximum(entries, -limit), limit).astype(kind)


def setup_inputs(seed: int = 0) -> dict:
    key_list = jax.random.split(jax.random.key(seed), 12)
    return {
        "multipoles": noise(key_list[0], (BOXES, P_SIZE), 1.0, 6.0, ((0, 64),)),
        "kernels": noise(key_list[1], (CLASSES, P_SIZE, P_SIZE), (CLASSES * P_SIZE) ** -0.5, 0.0390625, ((0, 4),)),
        "transfer": noise(key_list[2], (8, P_SIZE, P_SIZE), (8 * P_SIZE) ** -0.5, 0.09375),
        "leaf_target": draw_leaf_target(jax.random.fold_in(key_list[11], 71), 0),
        "leaf_source": draw_leaf_source(jax.random.fold_in(key_list[11], 71), 0),
        "leaf_count": draw_leaf_count(jax.random.fold_in(key_list[11], 71), 0),
        "coarse_target": draw_coarse_target(jax.random.fold_in(key_list[11], 71), 0),
        "coarse_source": draw_coarse_source(jax.random.fold_in(key_list[11], 71), 0),
        "coarse_count": draw_coarse_count(jax.random.fold_in(key_list[11], 71), 0),
        "ghost_send": draw_ghost_send(jax.random.fold_in(key_list[11], 71), 0),
        "coarse_send": draw_coarse_send(jax.random.fold_in(key_list[11], 71), 0),
    }


def align(target, source, pair_count, pad_row):
    slot_count = target.shape[0]
    is_valid = jnp.arange(slot_count) < pair_count
    target_slot = jnp.where(is_valid, target, slot_count)
    return jnp.full((slot_count,), pad_row, jnp.int32).at[target_slot].set(source.astype(jnp.int32), mode="drop")


def hypercube(owned, send_lists):
    buffer = owned
    for bit_index in range(ROUNDS):
        picked = jax.vmap(lambda block, chosen: block[chosen])(buffer, send_lists[:, bit_index])
        partner = jnp.arange(N_LEAF) ^ (1 << bit_index)
        buffer = jnp.concatenate([buffer, picked[partner]], axis=1)
    return buffer


def far_field(buffer, kernel_flat, target, source, pair_count):
    padded = jnp.concatenate([buffer, jnp.zeros((1, buffer.shape[1]), buffer.dtype)], axis=0)
    slot_index = jax.vmap(align, in_axes=(0, 0, 0, None))(target, source, pair_count, buffer.shape[0])
    aligned = padded[slot_index.T]
    flat = aligned.reshape(aligned.shape[0], -1)
    return jnp.dot(flat, kernel_flat, preferred_element_type=jnp.float32)


def spread_down(coarse_local, transfer):
    coarse_high = coarse_local.astype(jnp.bfloat16)
    coarse_low = (coarse_local - coarse_high.astype(jnp.float32)).astype(jnp.bfloat16)
    transfer_wide = transfer.astype(jnp.float32)
    high_part = jnp.einsum("jq,opq->jop", coarse_high.astype(jnp.float32), transfer_wide, precision=lax.Precision.HIGHEST)
    low_part = jnp.einsum("jq,opq->jop", coarse_low.astype(jnp.float32), transfer_wide, precision=lax.Precision.HIGHEST)
    return (high_part + low_part).reshape(-1, transfer.shape[1])


def reference(multipoles, kernels, transfer, leaf_target, leaf_source, leaf_count, coarse_target, coarse_source, coarse_count, ghost_send, coarse_send):
    width = multipoles.shape[1]
    parent = jnp.dot(multipoles.reshape(-1, 8 * width), transfer.reshape(8 * width, width), preferred_element_type=jnp.float32).astype(jnp.bfloat16)
    buffer = hypercube(multipoles.reshape(N_LEAF, BOX_DEV, width), ghost_send)
    coarse_buffer = hypercube(parent.reshape(N_LEAF, PAR_DEV, width), coarse_send)
    kernel_flat = kernels.reshape(CLASSES * width, width)

    def partition(items):
        leaf_rows, parent_rows, ltarget, lsource, lcount, ctarget, csource, ccount = items
        leaf_part = far_field(leaf_rows, kernel_flat, ltarget, lsource, lcount)
        coarse_local = 0.5 * far_field(parent_rows, kernel_flat, ctarget, csource, ccount)
        return leaf_part + spread_down(coarse_local, transfer)

    result = lax.map(partition, (buffer, coarse_buffer, leaf_target, leaf_source, leaf_count, coarse_target, coarse_source, coarse_count))
    return result.reshape(BOXES, width)
```

```python
import jax
import jax.numpy as jnp
from jax import lax
from jax.sharding import PartitionSpec as P


def partner(block, axis, apart):
    count = lax.axis_size(axis)
    route = []
    for low in range(count):
        high = low | 1 << apart
        if high != low and high < count:
            route += [(low, high), (high, low)]
    return lax.ppermute(block, axis, route)


def slot_table(target, source, pair_count, pad_row):
    pair = lax.broadcasted_iota(jnp.int32, target.shape, 1)
    payload = jnp.where(pair < pair_count[:, None], source, pad_row)
    _, slot = lax.sort((target, payload), dimension=1, num_keys=1)
    return slot


def class_sum(buffer, slot, kernels):
    width = buffer.shape[1]
    aligned = buffer.at[slot.T].get(mode="fill", fill_value=0)
    flat = aligned.reshape(aligned.shape[0], -1)
    return jnp.dot(flat, kernels.reshape(-1, width), preferred_element_type=jnp.float32)


def spread_down(coarse_local, transfer):
    coarse_high = coarse_local.astype(jnp.bfloat16)
    coarse_low = (coarse_local - coarse_high.astype(jnp.float32)).astype(jnp.bfloat16)
    high_part = jnp.einsum("jq,opq->jop", coarse_high, transfer, preferred_element_type=jnp.float32)
    low_part = jnp.einsum("jq,opq->jop", coarse_low, transfer, preferred_element_type=jnp.float32)
    return (high_part + low_part).reshape(-1, transfer.shape[1])


def exchange(owned, send, rows_per_round, rounds):
    width = owned.shape[1]
    total = owned.shape[0] + rounds * rows_per_round
    buffer = jnp.zeros((total, width), owned.dtype)
    buffer = lax.dynamic_update_slice(buffer, owned, (0, 0))
    for bit_index in range(rounds):
        arrived = partner(buffer[send[0, bit_index]], "leaf", bit_index)
        at = owned.shape[0] + bit_index * rows_per_round
        buffer = lax.dynamic_update_slice(buffer, arrived, (at, 0))
    return buffer


def on_device(
    multipoles,
    kernels,
    transfer,
    leaf_target,
    leaf_source,
    leaf_count,
    coarse_target,
    coarse_source,
    coarse_count,
    ghost_send,
    coarse_send,
):
    width = multipoles.shape[1]
    rounds = lax.axis_size("leaf").bit_length() - 1
    parent = jnp.dot(
        multipoles.reshape(-1, 8 * width),
        transfer.reshape(8 * width, width),
        preferred_element_type=jnp.float32,
    ).astype(jnp.bfloat16)
    buffer = exchange(multipoles, ghost_send, ghost_send.shape[2], rounds)
    coarse_buffer = exchange(parent, coarse_send, coarse_send.shape[2], rounds)
    leaf_slot = slot_table(leaf_target[0], leaf_source[0], leaf_count[0], buffer.shape[0])
    coarse_slot = slot_table(coarse_target[0], coarse_source[0], coarse_count[0], coarse_buffer.shape[0])
    coarse_local = 0.5 * class_sum(coarse_buffer, coarse_slot, kernels)
    partial_sum = class_sum(buffer, leaf_slot, kernels) + spread_down(coarse_local, transfer)
    return lax.psum_scatter(partial_sum, "off", scatter_dimension=0, tiled=True)


def solution(mesh):
    in_specs = (
        P("leaf", None),
        P("off", None, None),
        P(),
        P("leaf", "off", None),
        P("leaf", "off", None),
        P("leaf", "off"),
        P("leaf", "off", None),
        P("leaf", "off", None),
        P("leaf", "off"),
        P("leaf", None, None),
        P("leaf", None, None),
    )
    out_specs = P(("leaf", "off"), None)
    return jax.shard_map(
        on_device, mesh=mesh, in_specs=in_specs, out_specs=out_specs, check_vma=False
    )
```

```python
import jax
import jax.numpy as jnp
from jax import lax
from jax.sharding import PartitionSpec as P

LANES = 512


def partner(block, axis, apart):
    count = lax.axis_size(axis)
    route = []
    for low in range(count):
        high = low | 1 << apart
        if high != low and high < count:
            route += [(low, high), (high, low)]
    return lax.ppermute(block, axis, route)


def slot_table(target, source, pair_count, pad_row):
    pair = lax.broadcasted_iota(jnp.int32, target.shape, 1)
    payload = jnp.where(pair < pair_count[:, None], source, pad_row)
    _, slot = lax.sort((target, payload), dimension=1, num_keys=1)
    return slot


def widen(rows):
    return jnp.pad(rows, ((0, 0), (0, LANES - rows.shape[1])))


def select_rows(slot, first, rows):
    targets = slot.shape[1]
    ids = slot.T.reshape(-1, 1) - first
    hot = (ids == lax.broadcasted_iota(jnp.int32, (1, rows.shape[0]), 1)).astype(rows.dtype)
    picked = jnp.dot(hot, rows, preferred_element_type=jnp.float32).astype(rows.dtype)
    return picked.reshape(targets, -1)


def spread_down(coarse_local, transfer):
    coarse_high = coarse_local.astype(jnp.bfloat16)
    coarse_low = (coarse_local - coarse_high.astype(jnp.float32)).astype(jnp.bfloat16)
    high_part = jnp.einsum("jq,opq->jop", coarse_high, transfer, preferred_element_type=jnp.float32)
    low_part = jnp.einsum("jq,opq->jop", coarse_low, transfer, preferred_element_type=jnp.float32)
    return (high_part + low_part).reshape(-1, transfer.shape[1])


def on_device(
    multipoles,
    kernels,
    transfer,
    leaf_target,
    leaf_source,
    leaf_count,
    coarse_target,
    coarse_source,
    coarse_count,
    ghost_send,
    coarse_send,
):
    width = multipoles.shape[1]
    rounds = lax.axis_size("leaf").bit_length() - 1
    boxes = multipoles.shape[0]
    parents = boxes // 8
    leaf_ghost = ghost_send.shape[2]
    coarse_ghost = coarse_send.shape[2]
    leaf_rows = boxes + rounds * leaf_ghost
    coarse_rows = parents + rounds * coarse_ghost

    parent = jnp.dot(
        multipoles.reshape(-1, 8 * width),
        transfer.reshape(8 * width, width),
        preferred_element_type=jnp.float32,
    ).astype(jnp.bfloat16)

    leaf_slot = slot_table(leaf_target[0], leaf_source[0], leaf_count[0], leaf_rows)
    coarse_slot = slot_table(coarse_target[0], coarse_source[0], coarse_count[0], coarse_rows)
    kernel_flat = jnp.pad(kernels, ((0, 0), (0, LANES - width), (0, 0))).reshape(-1, width)

    own_wide = widen(multipoles)
    pieces = rounds - 1
    span = boxes // pieces // 8 * 8
    edges = [k * span for k in range(pieces)] + [boxes]
    own_pieces = []

    buffer = jnp.zeros((leaf_rows, width), multipoles.dtype)
    buffer = lax.dynamic_update_slice(buffer, multipoles, (0, 0))
    coarse_buffer = jnp.zeros((coarse_rows, width), parent.dtype)
    coarse_buffer = lax.dynamic_update_slice(coarse_buffer, parent, (0, 0))
    for bit_index in range(rounds):
        outgoing = jnp.concatenate(
            [buffer[ghost_send[0, bit_index]], coarse_buffer[coarse_send[0, bit_index]]], axis=0
        )
        if bit_index < pieces:
            source_rows, outgoing = lax.optimization_barrier((own_wide, outgoing))
        arrived = partner(outgoing, "leaf", bit_index)
        if bit_index < pieces:
            lo, hi = edges[bit_index], edges[bit_index + 1]
            piece = select_rows(leaf_slot[:, lo:hi], 0, source_rows)
            piece, arrived = lax.optimization_barrier((piece, arrived))
            own_pieces.append(piece)
        buffer = lax.dynamic_update_slice(
            buffer, arrived[:leaf_ghost], (boxes + bit_index * leaf_ghost, 0)
        )
        coarse_buffer = lax.dynamic_update_slice(
            coarse_buffer, arrived[leaf_ghost:], (parents + bit_index * coarse_ghost, 0)
        )

    coarse_aligned = select_rows(coarse_slot, 0, widen(coarse_buffer))
    coarse_local = 0.5 * jnp.dot(coarse_aligned, kernel_flat, preferred_element_type=jnp.float32)
    ghost_part = select_rows(leaf_slot, boxes, widen(buffer[boxes:]))
    own_part = jnp.concatenate(own_pieces, axis=0)
    leaf_local = jnp.dot(own_part + ghost_part, kernel_flat, preferred_element_type=jnp.float32)
    partial_sum = leaf_local + spread_down(coarse_local, transfer)
    return lax.psum_scatter(partial_sum, "off", scatter_dimension=0, tiled=True)


def solution(mesh):
    in_specs = (
        P("leaf", None),
        P("off", None, None),
        P(),
        P("leaf", "off", None),
        P("leaf", "off", None),
        P("leaf", "off"),
        P("leaf", "off", None),
        P("leaf", "off", None),
        P("leaf", "off"),
        P("leaf", None, None),
        P("leaf", None, None),
    )
    out_specs = P(("leaf", "off"), None)
    return jax.shard_map(
        on_device, mesh=mesh, in_specs=in_specs, out_specs=out_specs, check_vma=False
    )
```

```python
import functools

import jax
import jax.numpy as jnp
from jax import lax
from jax.experimental import pallas as pl
from jax.experimental.pallas import tpu as pltpu
from jax.sharding import PartitionSpec as P


def partner(block, axis, apart):
    count = lax.axis_size(axis)
    route = []
    for low in range(count):
        high = low | 1 << apart
        if high != low and high < count:
            route += [(low, high), (high, low)]
    return lax.ppermute(block, axis, route)


def slot_table(target, source, pair_count, pad_row):
    pair = lax.broadcasted_iota(jnp.int32, target.shape, 1)
    payload = jnp.where(pair < pair_count[:, None], source, pad_row)
    _, slot = lax.sort((target, payload), dimension=1, num_keys=1)
    return slot


def translate_kernel(spread, slot_ref, buf_ref, k_ref, *rest):
    if spread:
        high_ref, low_ref, t_ref, out_ref = rest
        nt = (((1,), (1,)), ((), ()))
        out_ref[...] = lax.dot_general(
            high_ref[...], t_ref[...], nt, preferred_element_type=jnp.float32
        ) + lax.dot_general(low_ref[...], t_ref[...], nt, preferred_element_type=jnp.float32)
    else:
        (out_ref,) = rest
        out_ref[...] = jnp.zeros(out_ref.shape, out_ref.dtype)
    rows = buf_ref.shape[0]
    tile = out_ref.shape[0]

    def one_class(c, carry):
        ids = slot_ref[c]
        hot = (ids == lax.broadcasted_iota(jnp.int32, (tile, rows), 1)).astype(buf_ref.dtype)
        picked = jnp.dot(hot, buf_ref[...], preferred_element_type=jnp.float32)
        out_ref[...] += jnp.dot(
            picked.astype(k_ref.dtype), k_ref[c], preferred_element_type=jnp.float32
        )
        return carry

    lax.fori_loop(0, k_ref.shape[0], one_class, 0)


def translate(slot, buffer, kernels, spread=None):
    groups, classes, tile, _ = slot.shape
    rows, width = buffer.shape
    in_specs = [
        pl.BlockSpec((None, classes, tile, 1), lambda g: (g, 0, 0, 0)),
        pl.BlockSpec((rows, width), lambda g: (0, 0)),
        pl.BlockSpec((classes, width, width), lambda g: (0, 0, 0)),
    ]
    operands = [slot, buffer, kernels]
    if spread is not None:
        high, low, transfer = spread
        in_specs += [
            pl.BlockSpec((tile, width), lambda g: (0, 0)),
            pl.BlockSpec((tile, width), lambda g: (0, 0)),
            pl.BlockSpec((None, width, width), lambda g: (g, 0, 0)),
        ]
        operands += [high, low, transfer]
    flops = 2 * groups * classes * tile * width * (rows + width)
    return pl.pallas_call(
        functools.partial(translate_kernel, spread is not None),
        grid=(groups,),
        in_specs=in_specs,
        out_specs=pl.BlockSpec((None, tile, width), lambda g: (g, 0, 0)),
        out_shape=jax.ShapeDtypeStruct((groups, tile, width), jnp.float32),
        compiler_params=pltpu.CompilerParams(vmem_limit_bytes=48 * 1024 * 1024),
        cost_estimate=pl.CostEstimate(
            flops=flops, bytes_accessed=2 * kernels.size + 2 * buffer.size, transcendentals=0
        ),
    )(*operands)


def on_device(
    multipoles,
    kernels,
    transfer,
    leaf_target,
    leaf_source,
    leaf_count,
    coarse_target,
    coarse_source,
    coarse_count,
    ghost_send,
    coarse_send,
):
    width = multipoles.shape[1]
    rounds = lax.axis_size("leaf").bit_length() - 1
    boxes = multipoles.shape[0]
    parents = boxes // 8
    classes = kernels.shape[0]
    leaf_ghost = ghost_send.shape[2]
    coarse_ghost = coarse_send.shape[2]
    leaf_rows = boxes + rounds * leaf_ghost
    coarse_rows = parents + rounds * coarse_ghost

    parent = jnp.dot(
        multipoles.reshape(-1, 8 * width),
        transfer.reshape(8 * width, width),
        preferred_element_type=jnp.float32,
    ).astype(jnp.bfloat16)

    leaf_slot = slot_table(leaf_target[0], leaf_source[0], leaf_count[0], leaf_rows)
    coarse_slot = slot_table(coarse_target[0], coarse_source[0], coarse_count[0], coarse_rows)
    leaf_slot = leaf_slot.reshape(classes, parents, 8).transpose(2, 0, 1)[..., None]
    coarse_slot = coarse_slot[None, :, :, None]

    buffer = jnp.zeros((leaf_rows, width), multipoles.dtype)
    buffer = lax.dynamic_update_slice(buffer, multipoles, (0, 0))
    coarse_buffer = jnp.zeros((coarse_rows, width), parent.dtype)
    coarse_buffer = lax.dynamic_update_slice(coarse_buffer, parent, (0, 0))
    for bit_index in range(rounds):
        outgoing = jnp.concatenate(
            [buffer[ghost_send[0, bit_index]], coarse_buffer[coarse_send[0, bit_index]]], axis=0
        )
        arrived = partner(outgoing, "leaf", bit_index)
        buffer = lax.dynamic_update_slice(
            buffer, arrived[:leaf_ghost], (boxes + bit_index * leaf_ghost, 0)
        )
        coarse_buffer = lax.dynamic_update_slice(
            coarse_buffer, arrived[leaf_ghost:], (parents + bit_index * coarse_ghost, 0)
        )

    coarse_local = 0.5 * translate(coarse_slot, coarse_buffer, kernels)[0]
    coarse_high = coarse_local.astype(jnp.bfloat16)
    coarse_low = (coarse_local - coarse_high.astype(jnp.float32)).astype(jnp.bfloat16)
    partial_sum = translate(leaf_slot, buffer, kernels, (coarse_high, coarse_low, transfer))
    mine = lax.psum_scatter(partial_sum, "off", scatter_dimension=1, tiled=True)
    return mine.transpose(1, 0, 2).reshape(-1, width)


def solution(mesh):
    in_specs = (
        P("leaf", None),
        P("off", None, None),
        P(),
        P("leaf", "off", None),
        P("leaf", "off", None),
        P("leaf", "off"),
        P("leaf", "off", None),
        P("leaf", "off", None),
        P("leaf", "off"),
        P("leaf", None, None),
        P("leaf", None, None),
    )
    out_specs = P(("leaf", "off"), None)
    return jax.shard_map(
        on_device, mesh=mesh, in_specs=in_specs, out_specs=out_specs, check_vma=False
    )
```

```python
import functools

import jax
import jax.numpy as jnp
from jax import lax
from jax.experimental import pallas as pl
from jax.experimental.pallas import tpu as pltpu
from jax.sharding import PartitionSpec as P


def partner(block, axis, apart):
    count = lax.axis_size(axis)
    route = []
    for low in range(count):
        high = low | 1 << apart
        if high != low and high < count:
            route += [(low, high), (high, low)]
    return lax.ppermute(block, axis, route)


def slot_table(target, source, pair_count, pad_row):
    pair = lax.broadcasted_iota(jnp.int32, target.shape, 1)
    payload = jnp.where(pair < pair_count[:, None], source, pad_row)
    _, slot = lax.sort((target, payload), dimension=1, num_keys=1)
    return slot


def translate_kernel(spread, devices, slot_ref, buf_ref, k_ref, *rest):
    if spread:
        high_ref, low_ref, t_ref, out_ref = rest
        nt = (((1,), (1,)), ((), ()))
        octants = t_ref.shape[0]
        span = high_ref.shape[0] // devices
        for h in range(octants):
            term = lax.dot_general(
                high_ref[...], t_ref[h], nt, preferred_element_type=jnp.float32
            ) + lax.dot_general(low_ref[...], t_ref[h], nt, preferred_element_type=jnp.float32)
            for d in range(devices):
                at = (d * octants + h) * span
                out_ref[at:at + span, :] = term[d * span:(d + 1) * span]
    else:
        (out_ref,) = rest
        out_ref[...] = jnp.zeros(out_ref.shape, out_ref.dtype)
    rows = buf_ref.shape[0]
    tile = out_ref.shape[0]
    columns = jnp.transpose(slot_ref[...])
    for c in range(k_ref.shape[0]):
        ids = columns[:, c:c + 1]
        hot = (ids == lax.broadcasted_iota(jnp.int32, (tile, rows), 1)).astype(buf_ref.dtype)
        picked = jnp.dot(hot, buf_ref[...], preferred_element_type=jnp.float32)
        out_ref[...] += jnp.dot(
            picked.astype(k_ref.dtype), k_ref[c], preferred_element_type=jnp.float32
        )


def translate(slot, buffer, kernels, chunk, tile, spread=None, devices=1):
    classes = kernels.shape[0]
    rows, width = buffer.shape
    in_specs = [
        pl.BlockSpec((slot.shape[0], tile), lambda g: (0, chunk)),
        pl.BlockSpec((rows, width), lambda g: (0, 0)),
        pl.BlockSpec((classes, width, width), lambda g: (0, 0, 0)),
    ]
    operands = [slot, buffer, kernels]
    if spread is not None:
        high, low, transfer = spread
        octants = tile // high.shape[0]
        in_specs += [
            pl.BlockSpec(high.shape, lambda g: (0, 0)),
            pl.BlockSpec(low.shape, lambda g: (0, 0)),
            pl.BlockSpec((octants, width, width), lambda g: (chunk, 0, 0)),
        ]
        operands += [high, low, transfer]
    flops = 2 * classes * tile * width * (rows + width)
    return pl.pallas_call(
        functools.partial(translate_kernel, spread is not None, devices),
        grid=(1,),
        in_specs=in_specs,
        out_specs=pl.BlockSpec((tile, width), lambda g: (0, 0)),
        out_shape=jax.ShapeDtypeStruct((tile, width), jnp.float32),
        compiler_params=pltpu.CompilerParams(vmem_limit_bytes=48 * 1024 * 1024),
        cost_estimate=pl.CostEstimate(
            flops=flops, bytes_accessed=2 * kernels.size + 2 * buffer.size, transcendentals=0
        ),
    )(*operands)


def on_device(
    multipoles,
    kernels,
    transfer,
    leaf_target,
    leaf_source,
    leaf_count,
    coarse_target,
    coarse_source,
    coarse_count,
    ghost_send,
    coarse_send,
):
    width = multipoles.shape[1]
    rounds = lax.axis_size("leaf").bit_length() - 1
    boxes = multipoles.shape[0]
    parents = boxes // 8
    classes = kernels.shape[0]
    leaf_ghost = ghost_send.shape[2]
    coarse_ghost = coarse_send.shape[2]
    leaf_rows = boxes + rounds * leaf_ghost
    coarse_rows = parents + rounds * coarse_ghost

    parent = jnp.dot(
        multipoles.reshape(-1, 8 * width),
        transfer.reshape(8 * width, width),
        preferred_element_type=jnp.float32,
    ).astype(jnp.bfloat16)

    leaf_slot = slot_table(leaf_target[0], leaf_source[0], leaf_count[0], leaf_rows)
    coarse_slot = slot_table(coarse_target[0], coarse_source[0], coarse_count[0], coarse_rows)
    chunks = 4
    devices = lax.axis_size("off")
    span = parents // devices
    leaf_slot = leaf_slot.reshape(classes, devices, span, chunks, 8 // chunks)
    leaf_slot = leaf_slot.transpose(0, 3, 1, 4, 2).reshape(classes, boxes)
    leaf_slot = jnp.pad(leaf_slot, ((0, 16 - classes), (0, 0)), constant_values=leaf_rows)
    coarse_slot = jnp.pad(coarse_slot, ((0, 16 - classes), (0, 0)), constant_values=coarse_rows)

    buffer = jnp.zeros((leaf_rows, width), multipoles.dtype)
    buffer = lax.dynamic_update_slice(buffer, multipoles, (0, 0))
    coarse_buffer = jnp.zeros((coarse_rows, width), parent.dtype)
    coarse_buffer = lax.dynamic_update_slice(coarse_buffer, parent, (0, 0))
    for bit_index in range(rounds):
        outgoing = jnp.concatenate(
            [buffer[ghost_send[0, bit_index]], coarse_buffer[coarse_send[0, bit_index]]], axis=0
        )
        arrived = partner(outgoing, "leaf", bit_index)
        buffer = lax.dynamic_update_slice(
            buffer, arrived[:leaf_ghost], (boxes + bit_index * leaf_ghost, 0)
        )
        coarse_buffer = lax.dynamic_update_slice(
            coarse_buffer, arrived[leaf_ghost:], (parents + bit_index * coarse_ghost, 0)
        )

    coarse_local = 0.5 * translate(coarse_slot, coarse_buffer, kernels, 0, parents)
    coarse_high = coarse_local.astype(jnp.bfloat16)
    coarse_low = (coarse_local - coarse_high.astype(jnp.float32)).astype(jnp.bfloat16)
    tile = boxes // chunks
    mine = []
    for chunk in range(chunks):
        partial_sum = translate(
            leaf_slot, buffer, kernels, chunk, tile, (coarse_high, coarse_low, transfer), devices
        )
        if mine:
            partial_sum, _ = lax.optimization_barrier((partial_sum, mine[-1]))
        mine.append(lax.psum_scatter(partial_sum, "off", scatter_dimension=0, tiled=True))
    mine = jnp.stack(mine).reshape(8, span, width)
    return mine.transpose(1, 0, 2).reshape(-1, width)


def solution(mesh):
    in_specs = (
        P("leaf", None),
        P("off", None, None),
        P(),
        P("leaf", "off", None),
        P("leaf", "off", None),
        P("leaf", "off"),
        P("leaf", "off", None),
        P("leaf", "off", None),
        P("leaf", "off"),
        P("leaf", None, None),
        P("leaf", None, None),
    )
    out_specs = P(("leaf", "off"), None)
    return jax.shard_map(
        on_device, mesh=mesh, in_specs=in_specs, out_specs=out_specs, check_vma=False
    )
```

```python
import functools

import jax
import jax.numpy as jnp
from jax import lax
from jax.experimental import pallas as pl
from jax.experimental.pallas import tpu as pltpu
from jax.sharding import PartitionSpec as P


def partner(block, axis, apart):
    count = lax.axis_size(axis)
    route = []
    for low in range(count):
        high = low | 1 << apart
        if high != low and high < count:
            route += [(low, high), (high, low)]
    return lax.ppermute(block, axis, route)


def slot_table(target, source, pair_count, pad_row):
    pair = lax.broadcasted_iota(jnp.int32, target.shape, 1)
    payload = jnp.where(pair < pair_count[:, None], source, pad_row)
    _, slot = lax.sort((target, payload), dimension=1, num_keys=1)
    return slot


def translate_kernel(spread, devices, slot_ref, buf_ref, k_ref, *rest):
    if spread:
        high_ref, low_ref, t_ref, out_ref = rest
        nt = (((1,), (1,)), ((), ()))
        octants = t_ref.shape[0]
        span = high_ref.shape[0] // devices
        for h in range(octants):
            term = lax.dot_general(
                high_ref[...], t_ref[h], nt, preferred_element_type=jnp.float32
            ) + lax.dot_general(low_ref[...], t_ref[h], nt, preferred_element_type=jnp.float32)
            for d in range(devices):
                at = (d * octants + h) * span
                out_ref[at:at + span, :] = term[d * span:(d + 1) * span]
    else:
        (out_ref,) = rest
        out_ref[...] = jnp.zeros(out_ref.shape, out_ref.dtype)
    rows = buf_ref.shape[0]
    tile = out_ref.shape[0]
    columns = jnp.transpose(slot_ref[...])
    for c in range(k_ref.shape[0]):
        ids = columns[:, c:c + 1]
        hot = (ids == lax.broadcasted_iota(jnp.int32, (tile, rows), 1)).astype(buf_ref.dtype)
        picked = jnp.dot(hot, buf_ref[...], preferred_element_type=jnp.float32)
        out_ref[...] += jnp.dot(
            picked.astype(k_ref.dtype), k_ref[c], preferred_element_type=jnp.float32
        )


def translate(slot, buffer, kernels, chunk, tile, spread=None, devices=1):
    classes = kernels.shape[0]
    rows, width = buffer.shape
    in_specs = [
        pl.BlockSpec((slot.shape[0], tile), lambda g: (0, chunk)),
        pl.BlockSpec((rows, width), lambda g: (0, 0)),
        pl.BlockSpec((classes, width, width), lambda g: (0, 0, 0)),
    ]
    operands = [slot, buffer, kernels]
    if spread is not None:
        high, low, transfer = spread
        octants = tile // high.shape[0]
        in_specs += [
            pl.BlockSpec(high.shape, lambda g: (0, 0)),
            pl.BlockSpec(low.shape, lambda g: (0, 0)),
            pl.BlockSpec((octants, width, width), lambda g: (chunk, 0, 0)),
        ]
        operands += [high, low, transfer]
    flops = 2 * classes * tile * width * (rows + width)
    return pl.pallas_call(
        functools.partial(translate_kernel, spread is not None, devices),
        grid=(1,),
        in_specs=in_specs,
        out_specs=pl.BlockSpec((tile, width), lambda g: (0, 0)),
        out_shape=jax.ShapeDtypeStruct((tile, width), jnp.float32),
        compiler_params=pltpu.CompilerParams(vmem_limit_bytes=48 * 1024 * 1024),
        cost_estimate=pl.CostEstimate(
            flops=flops, bytes_accessed=2 * kernels.size + 2 * buffer.size, transcendentals=0
        ),
    )(*operands)


def on_device(
    multipoles,
    kernels,
    transfer,
    leaf_target,
    leaf_source,
    leaf_count,
    coarse_target,
    coarse_source,
    coarse_count,
    ghost_send,
    coarse_send,
):
    width = multipoles.shape[1]
    rounds = lax.axis_size("leaf").bit_length() - 1
    boxes = multipoles.shape[0]
    parents = boxes // 8
    classes = kernels.shape[0]
    leaf_ghost = ghost_send.shape[2]
    coarse_ghost = coarse_send.shape[2]
    leaf_rows = boxes + rounds * leaf_ghost
    coarse_rows = parents + rounds * coarse_ghost

    parent = jnp.dot(
        multipoles.reshape(-1, 8 * width),
        transfer.reshape(8 * width, width),
        preferred_element_type=jnp.float32,
    ).astype(jnp.bfloat16)

    leaf_slot = slot_table(leaf_target[0], leaf_source[0], leaf_count[0], leaf_rows)
    coarse_slot = slot_table(coarse_target[0], coarse_source[0], coarse_count[0], coarse_rows)
    chunks = 4
    devices = lax.axis_size("off")
    span = parents // devices
    leaf_slot = leaf_slot.reshape(classes, devices, span, chunks, 8 // chunks)
    leaf_slot = leaf_slot.transpose(0, 3, 1, 4, 2).reshape(classes, boxes)
    leaf_slot = jnp.pad(leaf_slot, ((0, 16 - classes), (0, 0)), constant_values=leaf_rows)
    coarse_slot = jnp.pad(coarse_slot, ((0, 16 - classes), (0, 0)), constant_values=coarse_rows)

    buffer = jnp.zeros((leaf_rows, width), multipoles.dtype)
    buffer = lax.dynamic_update_slice(buffer, multipoles, (0, 0))
    coarse_buffer = jnp.zeros((coarse_rows, width), parent.dtype)
    coarse_buffer = lax.dynamic_update_slice(coarse_buffer, parent, (0, 0))
    for bit_index in range(rounds):
        outgoing = jnp.concatenate(
            [buffer[ghost_send[0, bit_index]], coarse_buffer[coarse_send[0, bit_index]]], axis=0
        )
        arrived = partner(outgoing, "leaf", bit_index)
        buffer = lax.dynamic_update_slice(
            buffer, arrived[:leaf_ghost], (boxes + bit_index * leaf_ghost, 0)
        )
        coarse_buffer = lax.dynamic_update_slice(
            coarse_buffer, arrived[leaf_ghost:], (parents + bit_index * coarse_ghost, 0)
        )

    coarse_local = 0.5 * translate(coarse_slot, coarse_buffer, kernels, 0, parents)
    coarse_high = coarse_local.astype(jnp.bfloat16)
    coarse_low = (coarse_local - coarse_high.astype(jnp.float32)).astype(jnp.bfloat16)
    tile = boxes // chunks
    block = tile // devices
    me = lax.axis_index("off")
    mine = []
    for chunk in range(chunks):
        slot_in = leaf_slot
        if chunk >= 2:
            slot_in, _ = lax.optimization_barrier((leaf_slot, mine[chunk - 2]))
        partial_sum = translate(
            slot_in, buffer, kernels, chunk, tile, (coarse_high, coarse_low, transfer), devices
        )
        total = lax.dynamic_slice_in_dim(partial_sum, me * block, block, 0)
        for shift in range(1, devices):
            theirs = lax.rem(me + shift, devices)
            sent = lax.dynamic_slice_in_dim(partial_sum, theirs * block, block, 0)
            route = [(k, (k + shift) % devices) for k in range(devices)]
            total = total + lax.ppermute(sent, "off", route)
        mine.append(total)
    mine = jnp.stack(mine).reshape(8, span, width)
    return mine.transpose(1, 0, 2).reshape(-1, width)


def solution(mesh):
    in_specs = (
        P("leaf", None),
        P("off", None, None),
        P(),
        P("leaf", "off", None),
        P("leaf", "off", None),
        P("leaf", "off"),
        P("leaf", "off", None),
        P("leaf", "off", None),
        P("leaf", "off"),
        P("leaf", None, None),
        P("leaf", None, None),
    )
    out_specs = P(("leaf", "off"), None)
    return jax.shard_map(
        on_device, mesh=mesh, in_specs=in_specs, out_specs=out_specs, check_vma=False
    )
```

```python
import functools

import jax
import jax.numpy as jnp
from jax import lax
from jax.experimental import pallas as pl
from jax.experimental.pallas import tpu as pltpu
from jax.sharding import PartitionSpec as P


def partner(block, axis, apart):
    count = lax.axis_size(axis)
    route = []
    for low in range(count):
        high = low | 1 << apart
        if high != low and high < count:
            route += [(low, high), (high, low)]
    return lax.ppermute(block, axis, route)


def invert_kernel(pad_row, column, count_ref, target_ref, source_ref, out_ref):
    pairs = target_ref.shape[1]
    for c in range(target_ref.shape[0]):
        valid = count_ref[c]

        def one_pair(i, carry, c=c, valid=valid):
            t = target_ref[c, i]
            value = jnp.where(i < valid, source_ref[c, i], pad_row)
            out_ref[c, column(t)] = value
            return carry

        lax.fori_loop(0, pairs, one_pair, 0, unroll=8)


def slot_table(target, source, pair_count, pad_row, column):
    smem = pl.BlockSpec(memory_space=pltpu.SMEM)
    return pl.pallas_call(
        functools.partial(invert_kernel, pad_row, column),
        in_specs=[smem, smem, smem],
        out_specs=smem,
        out_shape=jax.ShapeDtypeStruct(target.shape, jnp.int32),
    )(pair_count, target, source)


def translate_kernel(spread, devices, slot_ref, buf_ref, k_ref, *rest):
    if spread:
        high_ref, low_ref, t_ref, out_ref = rest
        nt = (((1,), (1,)), ((), ()))
        octants = t_ref.shape[0]
        span = high_ref.shape[0] // devices
        for h in range(octants):
            term = lax.dot_general(
                high_ref[...], t_ref[h], nt, preferred_element_type=jnp.float32
            ) + lax.dot_general(low_ref[...], t_ref[h], nt, preferred_element_type=jnp.float32)
            for d in range(devices):
                at = (d * octants + h) * span
                out_ref[at:at + span, :] = term[d * span:(d + 1) * span]
    else:
        (out_ref,) = rest
        out_ref[...] = jnp.zeros(out_ref.shape, out_ref.dtype)
    rows = buf_ref.shape[0]
    tile = out_ref.shape[0]
    columns = jnp.transpose(slot_ref[...])
    for c in range(k_ref.shape[0]):
        ids = columns[:, c:c + 1]
        hot = (ids == lax.broadcasted_iota(jnp.int32, (tile, rows), 1)).astype(buf_ref.dtype)
        picked = jnp.dot(hot, buf_ref[...], preferred_element_type=jnp.float32)
        out_ref[...] += jnp.dot(
            picked.astype(k_ref.dtype), k_ref[c], preferred_element_type=jnp.float32
        )


def translate(slot, buffer, kernels, chunk, tile, spread=None, devices=1):
    classes = kernels.shape[0]
    rows, width = buffer.shape
    in_specs = [
        pl.BlockSpec((slot.shape[0], tile), lambda g: (0, chunk)),
        pl.BlockSpec((rows, width), lambda g: (0, 0)),
        pl.BlockSpec((classes, width, width), lambda g: (0, 0, 0)),
    ]
    operands = [slot, buffer, kernels]
    if spread is not None:
        high, low, transfer = spread
        octants = tile // high.shape[0]
        in_specs += [
            pl.BlockSpec(high.shape, lambda g: (0, 0)),
            pl.BlockSpec(low.shape, lambda g: (0, 0)),
            pl.BlockSpec((octants, width, width), lambda g: (chunk, 0, 0)),
        ]
        operands += [high, low, transfer]
    flops = 2 * classes * tile * width * (rows + width)
    return pl.pallas_call(
        functools.partial(translate_kernel, spread is not None, devices),
        grid=(1,),
        in_specs=in_specs,
        out_specs=pl.BlockSpec((tile, width), lambda g: (0, 0)),
        out_shape=jax.ShapeDtypeStruct((tile, width), jnp.float32),
        compiler_params=pltpu.CompilerParams(vmem_limit_bytes=48 * 1024 * 1024),
        cost_estimate=pl.CostEstimate(
            flops=flops, bytes_accessed=2 * kernels.size + 2 * buffer.size, transcendentals=0
        ),
    )(*operands)


def on_device(
    multipoles,
    kernels,
    transfer,
    leaf_target,
    leaf_source,
    leaf_count,
    coarse_target,
    coarse_source,
    coarse_count,
    ghost_send,
    coarse_send,
):
    width = multipoles.shape[1]
    rounds = lax.axis_size("leaf").bit_length() - 1
    boxes = multipoles.shape[0]
    parents = boxes // 8
    classes = kernels.shape[0]
    leaf_ghost = ghost_send.shape[2]
    coarse_ghost = coarse_send.shape[2]
    leaf_rows = boxes + rounds * leaf_ghost
    coarse_rows = parents + rounds * coarse_ghost

    parent = jnp.dot(
        multipoles.reshape(-1, 8 * width),
        transfer.reshape(8 * width, width),
        preferred_element_type=jnp.float32,
    ).astype(jnp.bfloat16)

    chunks = 4
    devices = lax.axis_size("off")
    span = parents // devices
    per = 8 // chunks

    def leaf_column(t):
        j, o = t // 8, t % 8
        d, i = j // span, j % span
        g, h = o // per, o % per
        return ((g * devices + d) * per + h) * span + i

    leaf_slot = slot_table(leaf_target[0], leaf_source[0], leaf_count[0], leaf_rows, leaf_column)
    coarse_slot = slot_table(
        coarse_target[0], coarse_source[0], coarse_count[0], coarse_rows, lambda t: t
    )
    leaf_slot = jnp.pad(leaf_slot, ((0, 16 - classes), (0, 0)), constant_values=leaf_rows)
    coarse_slot = jnp.pad(coarse_slot, ((0, 16 - classes), (0, 0)), constant_values=coarse_rows)

    buffer = jnp.zeros((leaf_rows, width), multipoles.dtype)
    buffer = lax.dynamic_update_slice(buffer, multipoles, (0, 0))
    coarse_buffer = jnp.zeros((coarse_rows, width), parent.dtype)
    coarse_buffer = lax.dynamic_update_slice(coarse_buffer, parent, (0, 0))
    for bit_index in range(rounds):
        outgoing = jnp.concatenate(
            [buffer[ghost_send[0, bit_index]], coarse_buffer[coarse_send[0, bit_index]]], axis=0
        )
        arrived = partner(outgoing, "leaf", bit_index)
        buffer = lax.dynamic_update_slice(
            buffer, arrived[:leaf_ghost], (boxes + bit_index * leaf_ghost, 0)
        )
        coarse_buffer = lax.dynamic_update_slice(
            coarse_buffer, arrived[leaf_ghost:], (parents + bit_index * coarse_ghost, 0)
        )

    coarse_local = 0.5 * translate(coarse_slot, coarse_buffer, kernels, 0, parents)
    coarse_high = coarse_local.astype(jnp.bfloat16)
    coarse_low = (coarse_local - coarse_high.astype(jnp.float32)).astype(jnp.bfloat16)
    tile = boxes // chunks
    block = tile // devices
    me = lax.axis_index("off")
    mine = []
    for chunk in range(chunks):
        slot_in = leaf_slot
        if chunk >= 2:
            slot_in, _ = lax.optimization_barrier((leaf_slot, mine[chunk - 2]))
        partial_sum = translate(
            slot_in, buffer, kernels, chunk, tile, (coarse_high, coarse_low, transfer), devices
        )
        total = lax.dynamic_slice_in_dim(partial_sum, me * block, block, 0)
        for shift in range(1, devices):
            theirs = lax.rem(me + shift, devices)
            sent = lax.dynamic_slice_in_dim(partial_sum, theirs * block, block, 0)
            route = [(k, (k + shift) % devices) for k in range(devices)]
            total = total + lax.ppermute(sent, "off", route)
        mine.append(total)
    mine = jnp.stack(mine).reshape(8, span, width)
    return mine.transpose(1, 0, 2).reshape(-1, width)


def solution(mesh):
    in_specs = (
        P("leaf", None),
        P("off", None, None),
        P(),
        P("leaf", "off", None),
        P("leaf", "off", None),
        P("leaf", "off"),
        P("leaf", "off", None),
        P("leaf", "off", None),
        P("leaf", "off"),
        P("leaf", None, None),
        P("leaf", None, None),
    )
    out_specs = P(("leaf", "off"), None)
    return jax.shard_map(
        on_device, mesh=mesh, in_specs=in_specs, out_specs=out_specs, check_vma=False
    )
```

```python
import functools

import jax
import jax.numpy as jnp
from jax import lax
from jax.experimental import pallas as pl
from jax.experimental.pallas import tpu as pltpu
from jax.sharding import PartitionSpec as P


def partner(block, axis, apart):
    count = lax.axis_size(axis)
    route = []
    for low in range(count):
        high = low | 1 << apart
        if high != low and high < count:
            route += [(low, high), (high, low)]
    return lax.ppermute(block, axis, route)


def invert_kernel(target_ref, payload_ref, out_ref):
    pairs = target_ref.shape[1]
    columns = jnp.transpose(target_ref[...])
    spots = lax.broadcasted_iota(jnp.int32, (pairs, pairs), 1)
    for c in range(payload_ref.shape[0]):
        hot = (columns[:, c:c + 1] == spots).astype(payload_ref.dtype)
        parts = jnp.dot(payload_ref[c], hot, preferred_element_type=jnp.float32)
        out_ref[c:c + 1, :] = (parts[0:1] * 64.0 + parts[1:2]).astype(jnp.int32)


def slot_table(target, source, pair_count, pad_row):
    classes, pairs = target.shape
    pair = lax.broadcasted_iota(jnp.int32, target.shape, 1)
    payload = jnp.where(pair < pair_count[:, None], source, pad_row)
    split = jnp.stack([payload // 64, payload % 64], axis=1).astype(jnp.bfloat16)
    split = jnp.pad(split, ((0, 0), (0, 6), (0, 0)))
    target = jnp.pad(target, ((0, 16 - classes), (0, 0)), constant_values=-1)
    return pl.pallas_call(
        invert_kernel,
        out_shape=jax.ShapeDtypeStruct((classes, pairs), jnp.int32),
        compiler_params=pltpu.CompilerParams(vmem_limit_bytes=48 * 1024 * 1024),
        cost_estimate=pl.CostEstimate(
            flops=2 * 8 * classes * pairs * pairs, bytes_accessed=24 * classes * pairs, transcendentals=0
        ),
    )(target, split)


def translate_kernel(spread, devices, slot_ref, buf_ref, k_ref, *rest):
    if spread:
        high_ref, low_ref, t_ref, out_ref = rest
        nt = (((1,), (1,)), ((), ()))
        octants = t_ref.shape[0]
        span = high_ref.shape[0] // devices
        for h in range(octants):
            term = lax.dot_general(
                high_ref[...], t_ref[h], nt, preferred_element_type=jnp.float32
            ) + lax.dot_general(low_ref[...], t_ref[h], nt, preferred_element_type=jnp.float32)
            for d in range(devices):
                at = (d * octants + h) * span
                out_ref[at:at + span, :] = term[d * span:(d + 1) * span]
    else:
        (out_ref,) = rest
        out_ref[...] = jnp.zeros(out_ref.shape, out_ref.dtype)
    rows = buf_ref.shape[0]
    tile = out_ref.shape[0]
    columns = jnp.transpose(slot_ref[...])
    for c in range(k_ref.shape[0]):
        ids = columns[:, c:c + 1]
        hot = (ids == lax.broadcasted_iota(jnp.int32, (tile, rows), 1)).astype(buf_ref.dtype)
        picked = jnp.dot(hot, buf_ref[...], preferred_element_type=jnp.float32)
        out_ref[...] += jnp.dot(
            picked.astype(k_ref.dtype), k_ref[c], preferred_element_type=jnp.float32
        )


def translate(slot, buffer, kernels, chunk, tile, spread=None, devices=1):
    classes = kernels.shape[0]
    rows, width = buffer.shape
    in_specs = [
        pl.BlockSpec((slot.shape[0], tile), lambda g: (0, chunk)),
        pl.BlockSpec((rows, width), lambda g: (0, 0)),
        pl.BlockSpec((classes, width, width), lambda g: (0, 0, 0)),
    ]
    operands = [slot, buffer, kernels]
    if spread is not None:
        high, low, transfer = spread
        octants = tile // high.shape[0]
        in_specs += [
            pl.BlockSpec(high.shape, lambda g: (0, 0)),
            pl.BlockSpec(low.shape, lambda g: (0, 0)),
            pl.BlockSpec((octants, width, width), lambda g: (chunk, 0, 0)),
        ]
        operands += [high, low, transfer]
    flops = 2 * classes * tile * width * (rows + width)
    return pl.pallas_call(
        functools.partial(translate_kernel, spread is not None, devices),
        grid=(1,),
        in_specs=in_specs,
        out_specs=pl.BlockSpec((tile, width), lambda g: (0, 0)),
        out_shape=jax.ShapeDtypeStruct((tile, width), jnp.float32),
        compiler_params=pltpu.CompilerParams(vmem_limit_bytes=48 * 1024 * 1024),
        cost_estimate=pl.CostEstimate(
            flops=flops, bytes_accessed=2 * kernels.size + 2 * buffer.size, transcendentals=0
        ),
    )(*operands)


def on_device(
    multipoles,
    kernels,
    transfer,
    leaf_target,
    leaf_source,
    leaf_count,
    coarse_target,
    coarse_source,
    coarse_count,
    ghost_send,
    coarse_send,
):
    width = multipoles.shape[1]
    rounds = lax.axis_size("leaf").bit_length() - 1
    boxes = multipoles.shape[0]
    parents = boxes // 8
    classes = kernels.shape[0]
    leaf_ghost = ghost_send.shape[2]
    coarse_ghost = coarse_send.shape[2]
    leaf_rows = boxes + rounds * leaf_ghost
    coarse_rows = parents + rounds * coarse_ghost

    parent = jnp.dot(
        multipoles.reshape(-1, 8 * width),
        transfer.reshape(8 * width, width),
        preferred_element_type=jnp.float32,
    ).astype(jnp.bfloat16)

    coarse_slot = slot_table(coarse_target[0], coarse_source[0], coarse_count[0], coarse_rows)
    chunks = 4
    devices = lax.axis_size("off")
    span = parents // devices
    per = 8 // chunks
    coarse_slot = jnp.pad(coarse_slot, ((0, 16 - classes), (0, 0)), constant_values=coarse_rows)

    buffer = jnp.zeros((leaf_rows, width), multipoles.dtype)
    buffer = lax.dynamic_update_slice(buffer, multipoles, (0, 0))
    coarse_buffer = jnp.zeros((coarse_rows, width), parent.dtype)
    coarse_buffer = lax.dynamic_update_slice(coarse_buffer, parent, (0, 0))
    group = -(-classes // (rounds - 1))
    groups = [(low, min(low + group, classes)) for low in range(0, classes, group)]
    slot_parts = []
    for bit_index in range(rounds):
        outgoing = jnp.concatenate(
            [buffer[ghost_send[0, bit_index]], coarse_buffer[coarse_send[0, bit_index]]], axis=0
        )
        if bit_index < len(groups):
            low, high = groups[bit_index]
            tables, outgoing = lax.optimization_barrier(
                ((leaf_target[0, low:high], leaf_source[0, low:high], leaf_count[0, low:high]), outgoing)
            )
        arrived = partner(outgoing, "leaf", bit_index)
        if bit_index < len(groups):
            part, arrived = lax.optimization_barrier((slot_table(*tables, leaf_rows), arrived))
            slot_parts.append(part)
        buffer = lax.dynamic_update_slice(
            buffer, arrived[:leaf_ghost], (boxes + bit_index * leaf_ghost, 0)
        )
        coarse_buffer = lax.dynamic_update_slice(
            coarse_buffer, arrived[leaf_ghost:], (parents + bit_index * coarse_ghost, 0)
        )

    leaf_slot = jnp.concatenate(slot_parts, axis=0)
    leaf_slot = leaf_slot.reshape(classes, devices, span, chunks, per)
    leaf_slot = leaf_slot.transpose(0, 3, 1, 4, 2).reshape(classes, boxes)
    leaf_slot = jnp.pad(leaf_slot, ((0, 16 - classes), (0, 0)), constant_values=leaf_rows)
    coarse_local = 0.5 * translate(coarse_slot, coarse_buffer, kernels, 0, parents)
    coarse_high = coarse_local.astype(jnp.bfloat16)
    coarse_low = (coarse_local - coarse_high.astype(jnp.float32)).astype(jnp.bfloat16)
    tile = boxes // chunks
    block = tile // devices
    me = lax.axis_index("off")
    mine = []
    for chunk in range(chunks):
        slot_in = leaf_slot
        if chunk >= 2:
            slot_in, _ = lax.optimization_barrier((leaf_slot, mine[chunk - 2]))
        partial_sum = translate(
            slot_in, buffer, kernels, chunk, tile, (coarse_high, coarse_low, transfer), devices
        )
        total = lax.dynamic_slice_in_dim(partial_sum, me * block, block, 0)
        for shift in range(1, devices):
            theirs = lax.rem(me + shift, devices)
            sent = lax.dynamic_slice_in_dim(partial_sum, theirs * block, block, 0)
            route = [(k, (k + shift) % devices) for k in range(devices)]
            total = total + lax.ppermute(sent, "off", route)
        mine.append(total)
    mine = jnp.stack(mine).reshape(8, span, width)
    return mine.transpose(1, 0, 2).reshape(-1, width)


def solution(mesh):
    in_specs = (
        P("leaf", None),
        P("off", None, None),
        P(),
        P("leaf", "off", None),
        P("leaf", "off", None),
        P("leaf", "off"),
        P("leaf", "off", None),
        P("leaf", "off", None),
        P("leaf", "off"),
        P("leaf", None, None),
        P("leaf", None, None),
    )
    out_specs = P(("leaf", "off"), None)
    return jax.shard_map(
        on_device, mesh=mesh, in_specs=in_specs, out_specs=out_specs, check_vma=False
    )
```

```python
import functools

import jax
import jax.numpy as jnp
from jax import lax
from jax.experimental import pallas as pl
from jax.experimental.pallas import tpu as pltpu
from jax.sharding import PartitionSpec as P


def partner(block, axis, apart):
    count = lax.axis_size(axis)
    route = []
    for low in range(count):
        high = low | 1 << apart
        if high != low and high < count:
            route += [(low, high), (high, low)]
    return lax.ppermute(block, axis, route)


def invert_kernel(target_ref, payload_ref, out_ref):
    pairs = target_ref.shape[1]
    columns = jnp.transpose(target_ref[...])
    spots = lax.broadcasted_iota(jnp.int32, (pairs, pairs), 1)
    for c in range(payload_ref.shape[0]):
        hot = (columns[:, c:c + 1] == spots).astype(payload_ref.dtype)
        parts = jnp.dot(payload_ref[c], hot, preferred_element_type=jnp.float32)
        out_ref[c:c + 1, :] = (parts[0:1] * 64.0 + parts[1:2]).astype(jnp.int32)


def slot_table(target, source, pair_count, pad_row):
    classes, pairs = target.shape
    pair = lax.broadcasted_iota(jnp.int32, target.shape, 1)
    payload = jnp.where(pair < pair_count[:, None], source, pad_row)
    split = jnp.stack([payload // 64, payload % 64], axis=1).astype(jnp.bfloat16)
    split = jnp.pad(split, ((0, 0), (0, 6), (0, 0)))
    target = jnp.pad(target, ((0, 16 - classes), (0, 0)), constant_values=-1)
    return pl.pallas_call(
        invert_kernel,
        out_shape=jax.ShapeDtypeStruct((classes, pairs), jnp.int32),
        compiler_params=pltpu.CompilerParams(vmem_limit_bytes=48 * 1024 * 1024),
        cost_estimate=pl.CostEstimate(
            flops=2 * 8 * classes * pairs * pairs, bytes_accessed=24 * classes * pairs, transcendentals=0
        ),
    )(target, split)


def translate_kernel(spread, devices, offset, has_base, slot_ref, buf_ref, k_ref, *rest):
    rest = list(rest)
    out_ref = rest.pop()
    base_ref = rest.pop(0) if has_base else None
    if spread:
        high_ref, low_ref, t_ref = rest
        nt = (((1,), (1,)), ((), ()))
        octants = t_ref.shape[0]
        span = high_ref.shape[0] // devices
        for h in range(octants):
            term = lax.dot_general(
                high_ref[...], t_ref[h], nt, preferred_element_type=jnp.float32
            ) + lax.dot_general(low_ref[...], t_ref[h], nt, preferred_element_type=jnp.float32)
            for d in range(devices):
                at = (d * octants + h) * span
                out_ref[at:at + span, :] = term[d * span:(d + 1) * span]
        if has_base:
            out_ref[...] += base_ref[...]
    elif has_base:
        out_ref[...] = base_ref[...]
    else:
        out_ref[...] = jnp.zeros(out_ref.shape, out_ref.dtype)
    rows = buf_ref.shape[0]
    tile = out_ref.shape[0]
    columns = jnp.transpose(slot_ref[...]) - offset
    for c in range(k_ref.shape[0]):
        ids = columns[:, c:c + 1]
        hot = (ids == lax.broadcasted_iota(jnp.int32, (tile, rows), 1)).astype(buf_ref.dtype)
        picked = jnp.dot(hot, buf_ref[...], preferred_element_type=jnp.float32)
        out_ref[...] += jnp.dot(
            picked.astype(k_ref.dtype), k_ref[c], preferred_element_type=jnp.float32
        )


def translate(slot, buffer, kernels, chunk, tile, spread=None, devices=1, offset=0, base=None):
    classes = kernels.shape[0]
    rows, width = buffer.shape
    in_specs = [
        pl.BlockSpec((slot.shape[0], tile), lambda g: (0, chunk)),
        pl.BlockSpec((rows, width), lambda g: (0, 0)),
        pl.BlockSpec((classes, width, width), lambda g: (0, 0, 0)),
    ]
    operands = [slot, buffer, kernels]
    if base is not None:
        in_specs.append(pl.BlockSpec((tile, width), lambda g: (chunk, 0)))
        operands.append(base)
    if spread is not None:
        high, low, transfer = spread
        octants = tile // high.shape[0]
        in_specs += [
            pl.BlockSpec(high.shape, lambda g: (0, 0)),
            pl.BlockSpec(low.shape, lambda g: (0, 0)),
            pl.BlockSpec((octants, width, width), lambda g: (chunk, 0, 0)),
        ]
        operands += [high, low, transfer]
    flops = 2 * classes * tile * width * (rows + width)
    kernel = functools.partial(
        translate_kernel, spread is not None, devices, offset, base is not None
    )
    return pl.pallas_call(
        kernel,
        grid=(1,),
        in_specs=in_specs,
        out_specs=pl.BlockSpec((tile, width), lambda g: (0, 0)),
        out_shape=jax.ShapeDtypeStruct((tile, width), jnp.float32),
        compiler_params=pltpu.CompilerParams(vmem_limit_bytes=48 * 1024 * 1024),
        cost_estimate=pl.CostEstimate(
            flops=flops, bytes_accessed=2 * kernels.size + 2 * buffer.size, transcendentals=0
        ),
    )(*operands)


def on_device(
    multipoles,
    kernels,
    transfer,
    leaf_target,
    leaf_source,
    leaf_count,
    coarse_target,
    coarse_source,
    coarse_count,
    ghost_send,
    coarse_send,
):
    width = multipoles.shape[1]
    rounds = lax.axis_size("leaf").bit_length() - 1
    boxes = multipoles.shape[0]
    parents = boxes // 8
    classes = kernels.shape[0]
    leaf_ghost = ghost_send.shape[2]
    coarse_ghost = coarse_send.shape[2]
    leaf_rows = boxes + rounds * leaf_ghost
    coarse_rows = parents + rounds * coarse_ghost

    parent = jnp.dot(
        multipoles.reshape(-1, 8 * width),
        transfer.reshape(8 * width, width),
        preferred_element_type=jnp.float32,
    ).astype(jnp.bfloat16)

    coarse_slot = slot_table(coarse_target[0], coarse_source[0], coarse_count[0], coarse_rows)
    chunks = 4
    devices = lax.axis_size("off")
    span = parents // devices
    per = 8 // chunks
    coarse_slot = jnp.pad(coarse_slot, ((0, 16 - classes), (0, 0)), constant_values=coarse_rows)

    buffer = jnp.zeros((leaf_rows, width), multipoles.dtype)
    buffer = lax.dynamic_update_slice(buffer, multipoles, (0, 0))
    coarse_buffer = jnp.zeros((coarse_rows, width), parent.dtype)
    coarse_buffer = lax.dynamic_update_slice(coarse_buffer, parent, (0, 0))
    def reorder(table):
        count = table.shape[0]
        table = table.reshape(count, devices, span, chunks, per)
        return table.transpose(0, 3, 1, 4, 2).reshape(count, boxes)

    own_sum = jnp.zeros((boxes, width), jnp.float32)
    group = -(-classes // (rounds - 1))
    groups = [(low, min(low + group, classes)) for low in range(0, classes, group)]
    slot_parts = []
    for bit_index in range(rounds):
        outgoing = jnp.concatenate(
            [buffer[ghost_send[0, bit_index]], coarse_buffer[coarse_send[0, bit_index]]], axis=0
        )
        if bit_index < len(groups):
            low, high = groups[bit_index]
            tables, outgoing = lax.optimization_barrier(
                ((leaf_target[0, low:high], leaf_source[0, low:high], leaf_count[0, low:high]), outgoing)
            )
        if 0 < bit_index <= len(groups):
            low, high = groups[bit_index - 1]
            own_in, outgoing = lax.optimization_barrier(((slot_parts[-1], own_sum), outgoing))
            group_slot = jnp.pad(
                reorder(own_in[0]), ((0, 8 - (high - low)), (0, 0)), constant_values=leaf_rows
            )
            own_next = translate(group_slot, multipoles, kernels[low:high], 0, boxes, base=own_in[1])
        arrived = partner(outgoing, "leaf", bit_index)
        if bit_index < len(groups):
            part, arrived = lax.optimization_barrier((slot_table(*tables, leaf_rows), arrived))
            slot_parts.append(part)
        if 0 < bit_index <= len(groups):
            own_sum, arrived = lax.optimization_barrier((own_next, arrived))
        buffer = lax.dynamic_update_slice(
            buffer, arrived[:leaf_ghost], (boxes + bit_index * leaf_ghost, 0)
        )
        coarse_buffer = lax.dynamic_update_slice(
            coarse_buffer, arrived[leaf_ghost:], (parents + bit_index * coarse_ghost, 0)
        )

    leaf_slot = reorder(jnp.concatenate(slot_parts, axis=0))
    leaf_slot = jnp.pad(leaf_slot, ((0, 16 - classes), (0, 0)), constant_values=leaf_rows)
    coarse_local = 0.5 * translate(coarse_slot, coarse_buffer, kernels, 0, parents)
    coarse_high = coarse_local.astype(jnp.bfloat16)
    coarse_low = (coarse_local - coarse_high.astype(jnp.float32)).astype(jnp.bfloat16)
    tile = boxes // chunks
    block = tile // devices
    ghost_rows = buffer[boxes:]
    me = lax.axis_index("off")
    mine = []
    for chunk in range(chunks):
        slot_in = leaf_slot
        if chunk >= 2:
            slot_in, _ = lax.optimization_barrier((leaf_slot, mine[chunk - 2]))
        partial_sum = translate(
            slot_in, ghost_rows, kernels, chunk, tile, (coarse_high, coarse_low, transfer),
            devices, boxes, own_sum
        )
        total = lax.dynamic_slice_in_dim(partial_sum, me * block, block, 0)
        for shift in range(1, devices):
            theirs = lax.rem(me + shift, devices)
            sent = lax.dynamic_slice_in_dim(partial_sum, theirs * block, block, 0)
            route = [(k, (k + shift) % devices) for k in range(devices)]
            total = total + lax.ppermute(sent, "off", route)
        mine.append(total)
    mine = jnp.stack(mine).reshape(8, span, width)
    return mine.transpose(1, 0, 2).reshape(-1, width)


def solution(mesh):
    in_specs = (
        P("leaf", None),
        P("off", None, None),
        P(),
        P("leaf", "off", None),
        P("leaf", "off", None),
        P("leaf", "off"),
        P("leaf", "off", None),
        P("leaf", "off", None),
        P("leaf", "off"),
        P("leaf", None, None),
        P("leaf", None, None),
    )
    out_specs = P(("leaf", "off"), None)
    return jax.shard_map(
        on_device, mesh=mesh, in_specs=in_specs, out_specs=out_specs, check_vma=False
    )
```

```python
import functools

import jax
import jax.numpy as jnp
from jax import lax
from jax.experimental import pallas as pl
from jax.experimental.pallas import tpu as pltpu
from jax.sharding import PartitionSpec as P


def partner(block, axis, apart):
    count = lax.axis_size(axis)
    route = []
    for low in range(count):
        high = low | 1 << apart
        if high != low and high < count:
            route += [(low, high), (high, low)]
    return lax.ppermute(block, axis, route)


def invert_kernel(target_ref, payload_ref, out_ref):
    pairs = target_ref.shape[1]
    columns = jnp.transpose(target_ref[...])
    spots = lax.broadcasted_iota(jnp.int32, (pairs, pairs), 1)
    for c in range(payload_ref.shape[0]):
        hot = (columns[:, c:c + 1] == spots).astype(payload_ref.dtype)
        parts = jnp.dot(payload_ref[c], hot, preferred_element_type=jnp.float32)
        out_ref[c:c + 1, :] = (parts[0:1] * 64.0 + parts[1:2]).astype(jnp.int32)


def slot_table(target, source, pair_count, pad_row):
    classes, pairs = target.shape
    pair = lax.broadcasted_iota(jnp.int32, target.shape, 1)
    payload = jnp.where(pair < pair_count[:, None], source, pad_row)
    split = jnp.stack([payload // 64, payload % 64], axis=1).astype(jnp.bfloat16)
    split = jnp.pad(split, ((0, 0), (0, 6), (0, 0)))
    target = jnp.pad(target, ((0, 16 - classes), (0, 0)), constant_values=-1)
    return pl.pallas_call(
        invert_kernel,
        out_shape=jax.ShapeDtypeStruct((classes, pairs), jnp.int32),
        compiler_params=pltpu.CompilerParams(vmem_limit_bytes=48 * 1024 * 1024),
        cost_estimate=pl.CostEstimate(
            flops=2 * 8 * classes * pairs * pairs, bytes_accessed=24 * classes * pairs, transcendentals=0
        ),
    )(target, split)


def translate_kernel(spread, devices, slot_ref, buf_ref, k_ref, *rest):
    *rest, column_ref = rest
    if spread:
        high_ref, low_ref, t_ref, out_ref = rest
        nt = (((1,), (1,)), ((), ()))
        octants = t_ref.shape[0]
        span = high_ref.shape[0] // devices
        for h in range(octants):
            term = lax.dot_general(
                high_ref[...], t_ref[h], nt, preferred_element_type=jnp.float32
            ) + lax.dot_general(low_ref[...], t_ref[h], nt, preferred_element_type=jnp.float32)
            for d in range(devices):
                at = (d * octants + h) * span
                out_ref[at:at + span, :] = term[d * span:(d + 1) * span]
    else:
        (out_ref,) = rest
        out_ref[...] = jnp.zeros(out_ref.shape, out_ref.dtype)
    rows = buf_ref.shape[0]
    tile = out_ref.shape[0]
    columns = jnp.transpose(slot_ref[...])
    for c in range(k_ref.shape[0]):
        column_ref[c] = columns[:, c:c + 1]

    def one_class(c, carry):
        hot = (column_ref[c] == lax.broadcasted_iota(jnp.int32, (tile, rows), 1)).astype(
            buf_ref.dtype
        )
        picked = jnp.dot(hot, buf_ref[...], preferred_element_type=jnp.float32)
        out_ref[...] += jnp.dot(
            picked.astype(k_ref.dtype), k_ref[c], preferred_element_type=jnp.float32
        )
        return carry

    lax.fori_loop(0, k_ref.shape[0], one_class, 0)


def translate(slot, buffer, kernels, chunk, tile, spread=None, devices=1):
    classes = kernels.shape[0]
    rows, width = buffer.shape
    in_specs = [
        pl.BlockSpec((slot.shape[0], tile), lambda g: (0, chunk)),
        pl.BlockSpec((rows, width), lambda g: (0, 0)),
        pl.BlockSpec((classes, width, width), lambda g: (0, 0, 0)),
    ]
    operands = [slot, buffer, kernels]
    if spread is not None:
        high, low, transfer = spread
        octants = tile // high.shape[0]
        in_specs += [
            pl.BlockSpec(high.shape, lambda g: (0, 0)),
            pl.BlockSpec(low.shape, lambda g: (0, 0)),
            pl.BlockSpec((octants, width, width), lambda g: (chunk, 0, 0)),
        ]
        operands += [high, low, transfer]
    flops = 2 * classes * tile * width * (rows + width)
    return pl.pallas_call(
        functools.partial(translate_kernel, spread is not None, devices),
        grid=(1,),
        in_specs=in_specs,
        out_specs=pl.BlockSpec((tile, width), lambda g: (0, 0)),
        out_shape=jax.ShapeDtypeStruct((tile, width), jnp.float32),
        scratch_shapes=[pltpu.VMEM((slot.shape[0], tile, 1), jnp.int32)],
        compiler_params=pltpu.CompilerParams(vmem_limit_bytes=48 * 1024 * 1024),
        cost_estimate=pl.CostEstimate(
            flops=flops, bytes_accessed=2 * kernels.size + 2 * buffer.size, transcendentals=0
        ),
    )(*operands)


def on_device(
    multipoles,
    kernels,
    transfer,
    leaf_target,
    leaf_source,
    leaf_count,
    coarse_target,
    coarse_source,
    coarse_count,
    ghost_send,
    coarse_send,
):
    width = multipoles.shape[1]
    rounds = lax.axis_size("leaf").bit_length() - 1
    boxes = multipoles.shape[0]
    parents = boxes // 8
    classes = kernels.shape[0]
    leaf_ghost = ghost_send.shape[2]
    coarse_ghost = coarse_send.shape[2]
    leaf_rows = boxes + rounds * leaf_ghost
    coarse_rows = parents + rounds * coarse_ghost

    parent = jnp.dot(
        multipoles.reshape(-1, 8 * width),
        transfer.reshape(8 * width, width),
        preferred_element_type=jnp.float32,
    ).astype(jnp.bfloat16)

    coarse_slot = slot_table(coarse_target[0], coarse_source[0], coarse_count[0], coarse_rows)
    chunks = 4
    devices = lax.axis_size("off")
    span = parents // devices
    per = 8 // chunks
    coarse_slot = jnp.pad(coarse_slot, ((0, 16 - classes), (0, 0)), constant_values=coarse_rows)

    buffer = jnp.zeros((leaf_rows, width), multipoles.dtype)
    buffer = lax.dynamic_update_slice(buffer, multipoles, (0, 0))
    coarse_buffer = jnp.zeros((coarse_rows, width), parent.dtype)
    coarse_buffer = lax.dynamic_update_slice(coarse_buffer, parent, (0, 0))
    group = -(-classes // (rounds - 1))
    groups = [(low, min(low + group, classes)) for low in range(0, classes, group)]
    slot_parts = []
    for bit_index in range(rounds):
        outgoing = jnp.concatenate(
            [buffer[ghost_send[0, bit_index]], coarse_buffer[coarse_send[0, bit_index]]], axis=0
        )
        if bit_index < len(groups):
            low, high = groups[bit_index]
            tables, outgoing = lax.optimization_barrier(
                ((leaf_target[0, low:high], leaf_source[0, low:high], leaf_count[0, low:high]), outgoing)
            )
        arrived = partner(outgoing, "leaf", bit_index)
        if bit_index < len(groups):
            part, arrived = lax.optimization_barrier((slot_table(*tables, leaf_rows), arrived))
            slot_parts.append(part)
        buffer = lax.dynamic_update_slice(
            buffer, arrived[:leaf_ghost], (boxes + bit_index * leaf_ghost, 0)
        )
        coarse_buffer = lax.dynamic_update_slice(
            coarse_buffer, arrived[leaf_ghost:], (parents + bit_index * coarse_ghost, 0)
        )

    leaf_slot = jnp.concatenate(slot_parts, axis=0)
    leaf_slot = leaf_slot.reshape(classes, devices, span, chunks, per)
    leaf_slot = leaf_slot.transpose(0, 3, 1, 4, 2).reshape(classes, boxes)
    leaf_slot = jnp.pad(leaf_slot, ((0, 16 - classes), (0, 0)), constant_values=leaf_rows)
    coarse_local = 0.5 * translate(coarse_slot, coarse_buffer, kernels, 0, parents)
    coarse_high = coarse_local.astype(jnp.bfloat16)
    coarse_low = (coarse_local - coarse_high.astype(jnp.float32)).astype(jnp.bfloat16)
    tile = boxes // chunks
    block = tile // devices
    me = lax.axis_index("off")
    mine = []
    for chunk in range(chunks):
        slot_in = leaf_slot
        if chunk >= 2:
            slot_in, _ = lax.optimization_barrier((leaf_slot, mine[chunk - 2]))
        partial_sum = translate(
            slot_in, buffer, kernels, chunk, tile, (coarse_high, coarse_low, transfer), devices
        )
        total = lax.dynamic_slice_in_dim(partial_sum, me * block, block, 0)
        for shift in range(1, devices):
            theirs = lax.rem(me + shift, devices)
            sent = lax.dynamic_slice_in_dim(partial_sum, theirs * block, block, 0)
            route = [(k, (k + shift) % devices) for k in range(devices)]
            total = total + lax.ppermute(sent, "off", route)
        mine.append(total)
    mine = jnp.stack(mine).reshape(8, span, width)
    return mine.transpose(1, 0, 2).reshape(-1, width)


def solution(mesh):
    in_specs = (
        P("leaf", None),
        P("off", None, None),
        P(),
        P("leaf", "off", None),
        P("leaf", "off", None),
        P("leaf", "off"),
        P("leaf", "off", None),
        P("leaf", "off", None),
        P("leaf", "off"),
        P("leaf", None, None),
        P("leaf", None, None),
    )
    out_specs = P(("leaf", "off"), None)
    return jax.shard_map(
        on_device, mesh=mesh, in_specs=in_specs, out_specs=out_specs, check_vma=False
    )
```

```python
import functools

import jax
import jax.numpy as jnp
from jax import lax
from jax.experimental import pallas as pl
from jax.experimental.pallas import tpu as pltpu
from jax.sharding import PartitionSpec as P


def partner(block, axis, apart):
    count = lax.axis_size(axis)
    route = []
    for low in range(count):
        high = low | 1 << apart
        if high != low and high < count:
            route += [(low, high), (high, low)]
    return lax.ppermute(block, axis, route)


def invert_kernel(target_ref, payload_ref, out_ref):
    pairs = target_ref.shape[1]
    columns = jnp.transpose(target_ref[...])
    spots = lax.broadcasted_iota(jnp.int32, (pairs, pairs), 1)
    for c in range(payload_ref.shape[0]):
        hot = (columns[:, c:c + 1] == spots).astype(payload_ref.dtype)
        parts = jnp.dot(payload_ref[c], hot, preferred_element_type=jnp.float32)
        out_ref[c:c + 1, :] = (parts[0:1] * 64.0 + parts[1:2]).astype(jnp.int32)


def slot_table(target, source, pair_count, pad_row):
    classes, pairs = target.shape
    pair = lax.broadcasted_iota(jnp.int32, target.shape, 1)
    payload = jnp.where(pair < pair_count[:, None], source, pad_row)
    split = jnp.stack([payload // 64, payload % 64], axis=1).astype(jnp.bfloat16)
    split = jnp.pad(split, ((0, 0), (0, 6), (0, 0)))
    target = jnp.pad(target, ((0, 16 - classes), (0, 0)), constant_values=-1)
    return pl.pallas_call(
        invert_kernel,
        out_shape=jax.ShapeDtypeStruct((classes, pairs), jnp.int32),
        compiler_params=pltpu.CompilerParams(vmem_limit_bytes=48 * 1024 * 1024),
        cost_estimate=pl.CostEstimate(
            flops=2 * 8 * classes * pairs * pairs, bytes_accessed=24 * classes * pairs, transcendentals=0
        ),
    )(target, split)


def translate_kernel(spread, devices, slot_ref, buf_ref, k_ref, *rest):
    *rest, column_ref = rest
    if spread:
        high_ref, low_ref, t_ref, out_ref = rest
        nt = (((1,), (1,)), ((), ()))
        octants = t_ref.shape[0]
        span = high_ref.shape[0] // devices
        for h in range(octants):
            term = lax.dot_general(
                high_ref[...], t_ref[h], nt, preferred_element_type=jnp.float32
            ) + lax.dot_general(low_ref[...], t_ref[h], nt, preferred_element_type=jnp.float32)
            for d in range(devices):
                at = (d * octants + h) * span
                out_ref[at:at + span, :] = term[d * span:(d + 1) * span]
    else:
        (out_ref,) = rest
        out_ref[...] = jnp.zeros(out_ref.shape, out_ref.dtype)
    rows = buf_ref.shape[0]
    tile = out_ref.shape[0]
    columns = jnp.transpose(slot_ref[...])
    for c in range(k_ref.shape[0]):
        column_ref[c] = columns[:, c:c + 1]

    def one_class(c, carry):
        hot = (column_ref[c] == lax.broadcasted_iota(jnp.int32, (tile, rows), 1)).astype(
            buf_ref.dtype
        )
        picked = jnp.dot(hot, buf_ref[...], preferred_element_type=jnp.float32)
        out_ref[...] += jnp.dot(
            picked.astype(k_ref.dtype), k_ref[c], preferred_element_type=jnp.float32
        )
        return carry

    lax.fori_loop(0, k_ref.shape[0], one_class, 0, unroll=5)


def translate(slot, buffer, kernels, chunk, tile, spread=None, devices=1):
    classes = kernels.shape[0]
    rows, width = buffer.shape
    in_specs = [
        pl.BlockSpec((slot.shape[0], tile), lambda g: (0, chunk)),
        pl.BlockSpec((rows, width), lambda g: (0, 0)),
        pl.BlockSpec((classes, width, width), lambda g: (0, 0, 0)),
    ]
    operands = [slot, buffer, kernels]
    if spread is not None:
        high, low, transfer = spread
        octants = tile // high.shape[0]
        in_specs += [
            pl.BlockSpec(high.shape, lambda g: (0, 0)),
            pl.BlockSpec(low.shape, lambda g: (0, 0)),
            pl.BlockSpec((octants, width, width), lambda g: (chunk, 0, 0)),
        ]
        operands += [high, low, transfer]
    flops = 2 * classes * tile * width * (rows + width)
    return pl.pallas_call(
        functools.partial(translate_kernel, spread is not None, devices),
        grid=(1,),
        in_specs=in_specs,
        out_specs=pl.BlockSpec((tile, width), lambda g: (0, 0)),
        out_shape=jax.ShapeDtypeStruct((tile, width), jnp.float32),
        scratch_shapes=[pltpu.VMEM((slot.shape[0], tile, 1), jnp.int32)],
        compiler_params=pltpu.CompilerParams(vmem_limit_bytes=48 * 1024 * 1024),
        cost_estimate=pl.CostEstimate(
            flops=flops, bytes_accessed=2 * kernels.size + 2 * buffer.size, transcendentals=0
        ),
    )(*operands)


def on_device(
    multipoles,
    kernels,
    transfer,
    leaf_target,
    leaf_source,
    leaf_count,
    coarse_target,
    coarse_source,
    coarse_count,
    ghost_send,
    coarse_send,
):
    width = multipoles.shape[1]
    rounds = lax.axis_size("leaf").bit_length() - 1
    boxes = multipoles.shape[0]
    parents = boxes // 8
    classes = kernels.shape[0]
    leaf_ghost = ghost_send.shape[2]
    coarse_ghost = coarse_send.shape[2]
    leaf_rows = boxes + rounds * leaf_ghost
    coarse_rows = parents + rounds * coarse_ghost

    parent = jnp.dot(
        multipoles.reshape(-1, 8 * width),
        transfer.reshape(8 * width, width),
        preferred_element_type=jnp.float32,
    ).astype(jnp.bfloat16)

    coarse_slot = slot_table(coarse_target[0], coarse_source[0], coarse_count[0], coarse_rows)
    chunks = 4
    devices = lax.axis_size("off")
    span = parents // devices
    per = 8 // chunks
    coarse_slot = jnp.pad(coarse_slot, ((0, 16 - classes), (0, 0)), constant_values=coarse_rows)

    buffer = jnp.zeros((leaf_rows, width), multipoles.dtype)
    buffer = lax.dynamic_update_slice(buffer, multipoles, (0, 0))
    coarse_buffer = jnp.zeros((coarse_rows, width), parent.dtype)
    coarse_buffer = lax.dynamic_update_slice(coarse_buffer, parent, (0, 0))
    group = -(-classes // (rounds - 1))
    groups = [(low, min(low + group, classes)) for low in range(0, classes, group)]
    slot_parts = []
    for bit_index in range(rounds):
        outgoing = jnp.concatenate(
            [buffer[ghost_send[0, bit_index]], coarse_buffer[coarse_send[0, bit_index]]], axis=0
        )
        if bit_index < len(groups):
            low, high = groups[bit_index]
            tables, outgoing = lax.optimization_barrier(
                ((leaf_target[0, low:high], leaf_source[0, low:high], leaf_count[0, low:high]), outgoing)
            )
        arrived = partner(outgoing, "leaf", bit_index)
        if bit_index < len(groups):
            part, arrived = lax.optimization_barrier((slot_table(*tables, leaf_rows), arrived))
            slot_parts.append(part)
        buffer = lax.dynamic_update_slice(
            buffer, arrived[:leaf_ghost], (boxes + bit_index * leaf_ghost, 0)
        )
        coarse_buffer = lax.dynamic_update_slice(
            coarse_buffer, arrived[leaf_ghost:], (parents + bit_index * coarse_ghost, 0)
        )

    leaf_slot = jnp.concatenate(slot_parts, axis=0)
    leaf_slot = leaf_slot.reshape(classes, devices, span, chunks, per)
    leaf_slot = leaf_slot.transpose(0, 3, 1, 4, 2).reshape(classes, boxes)
    leaf_slot = jnp.pad(leaf_slot, ((0, 16 - classes), (0, 0)), constant_values=leaf_rows)
    coarse_local = 0.5 * translate(coarse_slot, coarse_buffer, kernels, 0, parents)
    coarse_high = coarse_local.astype(jnp.bfloat16)
    coarse_low = (coarse_local - coarse_high.astype(jnp.float32)).astype(jnp.bfloat16)
    tile = boxes // chunks
    block = tile // devices
    me = lax.axis_index("off")
    mine = []
    for chunk in range(chunks):
        slot_in = leaf_slot
        if chunk >= 2:
            slot_in, _ = lax.optimization_barrier((leaf_slot, mine[chunk - 2]))
        partial_sum = translate(
            slot_in, buffer, kernels, chunk, tile, (coarse_high, coarse_low, transfer), devices
        )
        total = lax.dynamic_slice_in_dim(partial_sum, me * block, block, 0)
        for shift in range(1, devices):
            theirs = lax.rem(me + shift, devices)
            sent = lax.dynamic_slice_in_dim(partial_sum, theirs * block, block, 0)
            route = [(k, (k + shift) % devices) for k in range(devices)]
            total = total + lax.ppermute(sent, "off", route)
        mine.append(total)
    mine = jnp.stack(mine).reshape(8, span, width)
    return mine.transpose(1, 0, 2).reshape(-1, width)


def solution(mesh):
    in_specs = (
        P("leaf", None),
        P("off", None, None),
        P(),
        P("leaf", "off", None),
        P("leaf", "off", None),
        P("leaf", "off"),
        P("leaf", "off", None),
        P("leaf", "off", None),
        P("leaf", "off"),
        P("leaf", None, None),
        P("leaf", None, None),
    )
    out_specs = P(("leaf", "off"), None)
    return jax.shard_map(
        on_device, mesh=mesh, in_specs=in_specs, out_specs=out_specs, check_vma=False
    )
```

```python
import functools

import jax
import jax.numpy as jnp
from jax import lax
from jax.experimental import pallas as pl
from jax.experimental.pallas import tpu as pltpu
from jax.sharding import PartitionSpec as P


def partner(block, axis, apart):
    count = lax.axis_size(axis)
    route = []
    for low in range(count):
        high = low | 1 << apart
        if high != low and high < count:
            route += [(low, high), (high, low)]
    return lax.ppermute(block, axis, route)


def invert_kernel(target_ref, payload_ref, out_ref):
    pairs = target_ref.shape[1]
    columns = jnp.transpose(target_ref[...])
    spots = lax.broadcasted_iota(jnp.int32, (pairs, pairs), 1)
    for c in range(payload_ref.shape[0]):
        hot = (columns[:, c:c + 1] == spots).astype(payload_ref.dtype)
        parts = jnp.dot(payload_ref[c], hot, preferred_element_type=jnp.float32)
        out_ref[c:c + 1, :] = (parts[0:1] * 64.0 + parts[1:2]).astype(jnp.int32)


def slot_table(target, source, pair_count, pad_row):
    classes, pairs = target.shape
    pair = lax.broadcasted_iota(jnp.int32, target.shape, 1)
    payload = jnp.where(pair < pair_count[:, None], source, pad_row)
    split = jnp.stack([payload // 64, payload % 64], axis=1).astype(jnp.bfloat16)
    split = jnp.pad(split, ((0, 0), (0, 6), (0, 0)))
    target = jnp.pad(target, ((0, 16 - classes), (0, 0)), constant_values=-1)
    return pl.pallas_call(
        invert_kernel,
        out_shape=jax.ShapeDtypeStruct((classes, pairs), jnp.int32),
        compiler_params=pltpu.CompilerParams(vmem_limit_bytes=48 * 1024 * 1024),
        cost_estimate=pl.CostEstimate(
            flops=2 * 8 * classes * pairs * pairs, bytes_accessed=24 * classes * pairs, transcendentals=0
        ),
    )(target, split)


def translate_kernel(spread, devices, slot_ref, buf_ref, k_ref, *rest):
    *rest, column_ref = rest
    if spread:
        high_ref, low_ref, t_ref, out_ref = rest
        nt = (((1,), (1,)), ((), ()))
        octants = t_ref.shape[0]
        span = high_ref.shape[0] // devices
        for h in range(octants):
            term = lax.dot_general(
                high_ref[...], t_ref[h], nt, preferred_element_type=jnp.float32
            ) + lax.dot_general(low_ref[...], t_ref[h], nt, preferred_element_type=jnp.float32)
            for d in range(devices):
                at = (d * octants + h) * span
                out_ref[at:at + span, :] = term[d * span:(d + 1) * span]
    else:
        (out_ref,) = rest
        out_ref[...] = jnp.zeros(out_ref.shape, out_ref.dtype)
    rows = buf_ref.shape[0]
    tile = out_ref.shape[0]
    columns = jnp.transpose(slot_ref[...])
    for c in range(k_ref.shape[0]):
        column_ref[c] = columns[:, c:c + 1]

    def one_class(c, carry):
        hot = (column_ref[c] == lax.broadcasted_iota(jnp.int32, (tile, rows), 1)).astype(
            buf_ref.dtype
        )
        picked = jnp.dot(hot, buf_ref[...], preferred_element_type=jnp.float32)
        out_ref[...] += jnp.dot(
            picked.astype(k_ref.dtype), k_ref[c], preferred_element_type=jnp.float32
        )
        return carry

    lax.fori_loop(0, k_ref.shape[0], one_class, 0, unroll=5)


def translate(slot, buffer, kernels, chunk, tile, spread=None, devices=1):
    classes = kernels.shape[0]
    rows, width = buffer.shape
    in_specs = [
        pl.BlockSpec((slot.shape[0], tile), lambda g: (0, chunk)),
        pl.BlockSpec((rows, width), lambda g: (0, 0)),
        pl.BlockSpec((classes, width, width), lambda g: (0, 0, 0)),
    ]
    operands = [slot, buffer, kernels]
    if spread is not None:
        high, low, transfer = spread
        octants = tile // high.shape[0]
        in_specs += [
            pl.BlockSpec(high.shape, lambda g: (0, 0)),
            pl.BlockSpec(low.shape, lambda g: (0, 0)),
            pl.BlockSpec((octants, width, width), lambda g: (chunk, 0, 0)),
        ]
        operands += [high, low, transfer]
    flops = 2 * classes * tile * width * (rows + width)
    return pl.pallas_call(
        functools.partial(translate_kernel, spread is not None, devices),
        grid=(1,),
        in_specs=in_specs,
        out_specs=pl.BlockSpec((tile, width), lambda g: (0, 0)),
        out_shape=jax.ShapeDtypeStruct((tile, width), jnp.float32),
        scratch_shapes=[pltpu.VMEM((slot.shape[0], tile, 1), jnp.int32)],
        compiler_params=pltpu.CompilerParams(vmem_limit_bytes=48 * 1024 * 1024),
        cost_estimate=pl.CostEstimate(
            flops=flops, bytes_accessed=2 * kernels.size + 2 * buffer.size, transcendentals=0
        ),
    )(*operands)


def on_device(
    multipoles,
    kernels,
    transfer,
    leaf_target,
    leaf_source,
    leaf_count,
    coarse_target,
    coarse_source,
    coarse_count,
    ghost_send,
    coarse_send,
):
    width = multipoles.shape[1]
    rounds = lax.axis_size("leaf").bit_length() - 1
    boxes = multipoles.shape[0]
    parents = boxes // 8
    classes = kernels.shape[0]
    leaf_ghost = ghost_send.shape[2]
    coarse_ghost = coarse_send.shape[2]
    leaf_rows = boxes + rounds * leaf_ghost
    coarse_rows = parents + rounds * coarse_ghost

    child = 8 * lax.broadcasted_iota(jnp.int32, (16, parents), 1) + lax.broadcasted_iota(
        jnp.int32, (16, parents), 0
    )
    child = jnp.where(child % 8 == lax.broadcasted_iota(jnp.int32, (16, parents), 0), child, boxes)
    parent = translate(child, multipoles, transfer, 0, parents).astype(jnp.bfloat16)

    coarse_slot = slot_table(coarse_target[0], coarse_source[0], coarse_count[0], coarse_rows)
    chunks = 4
    devices = lax.axis_size("off")
    span = parents // devices
    per = 8 // chunks
    coarse_slot = jnp.pad(coarse_slot, ((0, 16 - classes), (0, 0)), constant_values=coarse_rows)

    buffer = jnp.zeros((leaf_rows, width), multipoles.dtype)
    buffer = lax.dynamic_update_slice(buffer, multipoles, (0, 0))
    coarse_buffer = jnp.zeros((coarse_rows, width), parent.dtype)
    coarse_buffer = lax.dynamic_update_slice(coarse_buffer, parent, (0, 0))
    group = -(-classes // (rounds - 1))
    groups = [(low, min(low + group, classes)) for low in range(0, classes, group)]
    slot_parts = []
    for bit_index in range(rounds):
        outgoing = jnp.concatenate(
            [buffer[ghost_send[0, bit_index]], coarse_buffer[coarse_send[0, bit_index]]], axis=0
        )
        if bit_index < len(groups):
            low, high = groups[bit_index]
            tables, outgoing = lax.optimization_barrier(
                ((leaf_target[0, low:high], leaf_source[0, low:high], leaf_count[0, low:high]), outgoing)
            )
        arrived = partner(outgoing, "leaf", bit_index)
        if bit_index < len(groups):
            part, arrived = lax.optimization_barrier((slot_table(*tables, leaf_rows), arrived))
            slot_parts.append(part)
        buffer = lax.dynamic_update_slice(
            buffer, arrived[:leaf_ghost], (boxes + bit_index * leaf_ghost, 0)
        )
        coarse_buffer = lax.dynamic_update_slice(
            coarse_buffer, arrived[leaf_ghost:], (parents + bit_index * coarse_ghost, 0)
        )

    leaf_slot = jnp.concatenate(slot_parts, axis=0)
    leaf_slot = leaf_slot.reshape(classes, devices, span, chunks, per)
    leaf_slot = leaf_slot.transpose(0, 3, 1, 4, 2).reshape(classes, boxes)
    leaf_slot = jnp.pad(leaf_slot, ((0, 16 - classes), (0, 0)), constant_values=leaf_rows)
    coarse_local = 0.5 * translate(coarse_slot, coarse_buffer, kernels, 0, parents)
    coarse_high = coarse_local.astype(jnp.bfloat16)
    coarse_low = (coarse_local - coarse_high.astype(jnp.float32)).astype(jnp.bfloat16)
    tile = boxes // chunks
    block = tile // devices
    me = lax.axis_index("off")
    mine = []
    for chunk in range(chunks):
        slot_in = leaf_slot
        if chunk >= 2:
            slot_in, _ = lax.optimization_barrier((leaf_slot, mine[chunk - 2]))
        partial_sum = translate(
            slot_in, buffer, kernels, chunk, tile, (coarse_high, coarse_low, transfer), devices
        )
        total = lax.dynamic_slice_in_dim(partial_sum, me * block, block, 0)
        for shift in range(1, devices):
            theirs = lax.rem(me + shift, devices)
            sent = lax.dynamic_slice_in_dim(partial_sum, theirs * block, block, 0)
            route = [(k, (k + shift) % devices) for k in range(devices)]
            total = total + lax.ppermute(sent, "off", route)
        mine.append(total)
    mine = jnp.stack(mine).reshape(8, span, width)
    return mine.transpose(1, 0, 2).reshape(-1, width)


def solution(mesh):
    in_specs = (
        P("leaf", None),
        P("off", None, None),
        P(),
        P("leaf", "off", None),
        P("leaf", "off", None),
        P("leaf", "off"),
        P("leaf", "off", None),
        P("leaf", "off", None),
        P("leaf", "off"),
        P("leaf", None, None),
        P("leaf", None, None),
    )
    out_specs = P(("leaf", "off"), None)
    return jax.shard_map(
        on_device, mesh=mesh, in_specs=in_specs, out_specs=out_specs, check_vma=False
    )
```

```python
import functools

import jax
import jax.numpy as jnp
from jax import lax
from jax.experimental import pallas as pl
from jax.experimental.pallas import tpu as pltpu
from jax.sharding import PartitionSpec as P


def partner(block, axis, apart):
    count = lax.axis_size(axis)
    route = []
    for low in range(count):
        high = low | 1 << apart
        if high != low and high < count:
            route += [(low, high), (high, low)]
    return lax.ppermute(block, axis, route)


def invert_kernel(target_ref, payload_ref, out_ref):
    pairs = target_ref.shape[1]
    columns = jnp.transpose(target_ref[...])
    spots = lax.broadcasted_iota(jnp.int32, (pairs, pairs), 1)
    for c in range(payload_ref.shape[0]):
        hot = (columns[:, c:c + 1] == spots).astype(payload_ref.dtype)
        parts = jnp.dot(payload_ref[c], hot, preferred_element_type=jnp.float32)
        out_ref[c:c + 1, :] = (parts[0:1] * 64.0 + parts[1:2]).astype(jnp.int32)


def slot_table(target, source, pair_count, pad_row):
    classes, pairs = target.shape
    pair = lax.broadcasted_iota(jnp.int32, target.shape, 1)
    payload = jnp.where(pair < pair_count[:, None], source, pad_row)
    split = jnp.stack([payload // 64, payload % 64], axis=1).astype(jnp.bfloat16)
    split = jnp.pad(split, ((0, 0), (0, 6), (0, 0)))
    target = jnp.pad(target, ((0, 16 - classes), (0, 0)), constant_values=-1)
    return pl.pallas_call(
        invert_kernel,
        out_shape=jax.ShapeDtypeStruct((classes, pairs), jnp.int32),
        compiler_params=pltpu.CompilerParams(vmem_limit_bytes=48 * 1024 * 1024),
        cost_estimate=pl.CostEstimate(
            flops=2 * 8 * classes * pairs * pairs, bytes_accessed=24 * classes * pairs, transcendentals=0
        ),
    )(target, split)


def translate_kernel(spread, devices, slot_ref, buf_ref, k_ref, *rest):
    *rest, column_ref = rest
    if spread:
        high_ref, low_ref, t_ref, out_ref = rest
        nt = (((1,), (1,)), ((), ()))
        octants = t_ref.shape[0]
        span = high_ref.shape[0] // devices
        for h in range(octants):
            term = lax.dot_general(
                high_ref[...], t_ref[h], nt, preferred_element_type=jnp.float32
            ) + lax.dot_general(low_ref[...], t_ref[h], nt, preferred_element_type=jnp.float32)
            for d in range(devices):
                at = (d * octants + h) * span
                out_ref[at:at + span, :] = term[d * span:(d + 1) * span]
    else:
        (out_ref,) = rest
        out_ref[...] = jnp.zeros(out_ref.shape, out_ref.dtype)
    rows = buf_ref.shape[0]
    tile = out_ref.shape[0]
    columns = jnp.transpose(slot_ref[...])
    for c in range(k_ref.shape[0]):
        column_ref[c] = columns[:, c:c + 1]

    def one_class(c, carry):
        hot = (column_ref[c] == lax.broadcasted_iota(jnp.int32, (tile, rows), 1)).astype(
            buf_ref.dtype
        )
        picked = jnp.dot(hot, buf_ref[...], preferred_element_type=jnp.float32)
        out_ref[...] += jnp.dot(
            picked.astype(k_ref.dtype), k_ref[c], preferred_element_type=jnp.float32
        )
        return carry

    lax.fori_loop(0, k_ref.shape[0], one_class, 0, unroll=5)


def translate(slot, buffer, kernels, chunk, tile, spread=None, devices=1, rows=None, row_block=0):
    classes = kernels.shape[0]
    width = buffer.shape[1]
    rows = rows or buffer.shape[0]
    in_specs = [
        pl.BlockSpec((slot.shape[0], tile), lambda g: (0, chunk)),
        pl.BlockSpec((rows, width), lambda g: (row_block, 0)),
        pl.BlockSpec((classes, width, width), lambda g: (0, 0, 0)),
    ]
    operands = [slot, buffer, kernels]
    if spread is not None:
        high, low, transfer = spread
        octants = tile // high.shape[0]
        in_specs += [
            pl.BlockSpec(high.shape, lambda g: (0, 0)),
            pl.BlockSpec(low.shape, lambda g: (0, 0)),
            pl.BlockSpec((octants, width, width), lambda g: (chunk, 0, 0)),
        ]
        operands += [high, low, transfer]
    flops = 2 * classes * tile * width * (rows + width)
    return pl.pallas_call(
        functools.partial(translate_kernel, spread is not None, devices),
        grid=(1,),
        in_specs=in_specs,
        out_specs=pl.BlockSpec((tile, width), lambda g: (0, 0)),
        out_shape=jax.ShapeDtypeStruct((tile, width), jnp.float32),
        scratch_shapes=[pltpu.VMEM((slot.shape[0], tile, 1), jnp.int32)],
        compiler_params=pltpu.CompilerParams(vmem_limit_bytes=48 * 1024 * 1024),
        cost_estimate=pl.CostEstimate(
            flops=flops, bytes_accessed=2 * kernels.size + 2 * buffer.size, transcendentals=0
        ),
    )(*operands)


def on_device(
    multipoles,
    kernels,
    transfer,
    leaf_target,
    leaf_source,
    leaf_count,
    coarse_target,
    coarse_source,
    coarse_count,
    ghost_send,
    coarse_send,
):
    width = multipoles.shape[1]
    rounds = lax.axis_size("leaf").bit_length() - 1
    boxes = multipoles.shape[0]
    parents = boxes // 8
    classes = kernels.shape[0]
    leaf_ghost = ghost_send.shape[2]
    coarse_ghost = coarse_send.shape[2]
    leaf_rows = boxes + rounds * leaf_ghost
    coarse_rows = parents + rounds * coarse_ghost

    child = 8 * lax.broadcasted_iota(jnp.int32, (16, parents), 1) + lax.broadcasted_iota(
        jnp.int32, (16, parents), 0
    )
    child = jnp.where(child % 8 == lax.broadcasted_iota(jnp.int32, (16, parents), 0), child, boxes)
    parent = translate(child, multipoles, transfer, 0, parents).astype(jnp.bfloat16)

    coarse_slot = slot_table(coarse_target[0], coarse_source[0], coarse_count[0], coarse_rows)
    chunks = 4
    devices = lax.axis_size("off")
    span = parents // devices
    per = 8 // chunks
    coarse_slot = jnp.pad(coarse_slot, ((0, 16 - classes), (0, 0)), constant_values=coarse_rows)

    leaf_region = -(-leaf_rows // coarse_rows) * coarse_rows
    rows_all = jnp.zeros((leaf_region + coarse_rows, width), multipoles.dtype)
    rows_all = lax.dynamic_update_slice(rows_all, multipoles, (0, 0))
    rows_all = lax.dynamic_update_slice(rows_all, parent, (leaf_region, 0))
    group = -(-classes // (rounds - 1))
    groups = [(low, min(low + group, classes)) for low in range(0, classes, group)]
    slot_parts = []
    for bit_index in range(rounds):
        picks = jnp.concatenate([ghost_send[0, bit_index], coarse_send[0, bit_index] + leaf_region])
        outgoing = rows_all[picks]
        if bit_index < len(groups):
            low, high = groups[bit_index]
            tables, outgoing = lax.optimization_barrier(
                ((leaf_target[0, low:high], leaf_source[0, low:high], leaf_count[0, low:high]), outgoing)
            )
        arrived = partner(outgoing, "leaf", bit_index)
        if bit_index < len(groups):
            part, arrived = lax.optimization_barrier((slot_table(*tables, leaf_rows), arrived))
            slot_parts.append(part)
        rows_all = lax.dynamic_update_slice(
            rows_all, arrived[:leaf_ghost], (boxes + bit_index * leaf_ghost, 0)
        )
        rows_all = lax.dynamic_update_slice(
            rows_all, arrived[leaf_ghost:], (leaf_region + parents + bit_index * coarse_ghost, 0)
        )

    leaf_slot = jnp.concatenate(slot_parts, axis=0)
    leaf_slot = leaf_slot.reshape(classes, devices, span, chunks, per)
    leaf_slot = leaf_slot.transpose(0, 3, 1, 4, 2).reshape(classes, boxes)
    leaf_slot = jnp.pad(leaf_slot, ((0, 16 - classes), (0, 0)), constant_values=leaf_rows)
    coarse_local = 0.5 * translate(
        coarse_slot, rows_all, kernels, 0, parents, rows=coarse_rows, row_block=leaf_region // coarse_rows
    )
    coarse_high = coarse_local.astype(jnp.bfloat16)
    coarse_low = (coarse_local - coarse_high.astype(jnp.float32)).astype(jnp.bfloat16)
    tile = boxes // chunks
    block = tile // devices
    me = lax.axis_index("off")
    mine = []
    for chunk in range(chunks):
        slot_in = leaf_slot
        if chunk >= 2:
            slot_in, _ = lax.optimization_barrier((leaf_slot, mine[chunk - 2]))
        partial_sum = translate(
            slot_in, rows_all, kernels, chunk, tile, (coarse_high, coarse_low, transfer), devices,
            rows=leaf_rows,
        )
        total = lax.dynamic_slice_in_dim(partial_sum, me * block, block, 0)
        for shift in range(1, devices):
            theirs = lax.rem(me + shift, devices)
            sent = lax.dynamic_slice_in_dim(partial_sum, theirs * block, block, 0)
            route = [(k, (k + shift) % devices) for k in range(devices)]
            total = total + lax.ppermute(sent, "off", route)
        mine.append(total)
    mine = jnp.stack(mine).reshape(8, span, width)
    return mine.transpose(1, 0, 2).reshape(-1, width)


def solution(mesh):
    in_specs = (
        P("leaf", None),
        P("off", None, None),
        P(),
        P("leaf", "off", None),
        P("leaf", "off", None),
        P("leaf", "off"),
        P("leaf", "off", None),
        P("leaf", "off", None),
        P("leaf", "off"),
        P("leaf", None, None),
        P("leaf", None, None),
    )
    out_specs = P(("leaf", "off"), None)
    return jax.shard_map(
        on_device, mesh=mesh, in_specs=in_specs, out_specs=out_specs, check_vma=False
    )
```

```python
import functools

import jax
import jax.numpy as jnp
from jax import lax
from jax.experimental import pallas as pl
from jax.experimental.pallas import tpu as pltpu
from jax.sharding import PartitionSpec as P


def partner(block, axis, apart):
    count = lax.axis_size(axis)
    route = []
    for low in range(count):
        high = low | 1 << apart
        if high != low and high < count:
            route += [(low, high), (high, low)]
    return lax.ppermute(block, axis, route)


def invert_kernel(target_ref, payload_ref, out_ref):
    pairs = target_ref.shape[1]
    columns = jnp.transpose(target_ref[...])
    spots = lax.broadcasted_iota(jnp.int32, (pairs, pairs), 1)
    for c in range(payload_ref.shape[0]):
        hot = (columns[:, c:c + 1] == spots).astype(payload_ref.dtype)
        parts = jnp.dot(payload_ref[c], hot, preferred_element_type=jnp.float32)
        out_ref[c:c + 1, :] = (parts[0:1] * 64.0 + parts[1:2]).astype(jnp.int32)


def slot_table(target, source, pair_count, pad_row):
    classes, pairs = target.shape
    pair = lax.broadcasted_iota(jnp.int32, target.shape, 1)
    payload = jnp.where(pair < pair_count[:, None], source, pad_row)
    split = jnp.stack([payload // 64, payload % 64], axis=1).astype(jnp.bfloat16)
    split = jnp.pad(split, ((0, 0), (0, 6), (0, 0)))
    target = jnp.pad(target, ((0, 16 - classes), (0, 0)), constant_values=-1)
    return pl.pallas_call(
        invert_kernel,
        out_shape=jax.ShapeDtypeStruct((classes, pairs), jnp.int32),
        compiler_params=pltpu.CompilerParams(vmem_limit_bytes=48 * 1024 * 1024),
        cost_estimate=pl.CostEstimate(
            flops=2 * 8 * classes * pairs * pairs, bytes_accessed=24 * classes * pairs, transcendentals=0
        ),
    )(target, split)


def translate_kernel(spread, devices, slot_ref, buf_ref, k_ref, *rest):
    *rest, column_ref = rest
    if spread:
        high_ref, low_ref, t_ref, out_ref = rest
        nt = (((1,), (1,)), ((), ()))
        octants = t_ref.shape[0]
        span = high_ref.shape[0] // devices
        for h in range(octants):
            term = lax.dot_general(
                high_ref[...], t_ref[h], nt, preferred_element_type=jnp.float32
            ) + lax.dot_general(low_ref[...], t_ref[h], nt, preferred_element_type=jnp.float32)
            for d in range(devices):
                at = (d * octants + h) * span
                out_ref[at:at + span, :] = term[d * span:(d + 1) * span]
    else:
        (out_ref,) = rest
        out_ref[...] = jnp.zeros(out_ref.shape, out_ref.dtype)
    rows = buf_ref.shape[0]
    tile = out_ref.shape[0]
    columns = jnp.transpose(slot_ref[...])
    for c in range(k_ref.shape[0]):
        column_ref[c] = columns[:, c:c + 1]

    def one_class(c, carry):
        hot = (column_ref[c] == lax.broadcasted_iota(jnp.int32, (tile, rows), 1)).astype(
            buf_ref.dtype
        )
        picked = jnp.dot(hot, buf_ref[...], preferred_element_type=jnp.float32)
        out_ref[...] += jnp.dot(
            picked.astype(k_ref.dtype), k_ref[c], preferred_element_type=jnp.float32
        )
        return carry

    lax.fori_loop(0, k_ref.shape[0], one_class, 0, unroll=5)


def translate(slot, buffer, kernels, chunk, tile, spread=None, devices=1, rows=None, row_block=0):
    classes = kernels.shape[0]
    width = buffer.shape[1]
    rows = rows or buffer.shape[0]
    in_specs = [
        pl.BlockSpec((slot.shape[0], tile), lambda g: (0, chunk)),
        pl.BlockSpec((rows, width), lambda g: (row_block, 0)),
        pl.BlockSpec((classes, width, width), lambda g: (0, 0, 0)),
    ]
    operands = [slot, buffer, kernels]
    if spread is not None:
        high, low, transfer = spread
        octants = tile // high.shape[0]
        in_specs += [
            pl.BlockSpec(high.shape, lambda g: (0, 0)),
            pl.BlockSpec(low.shape, lambda g: (0, 0)),
            pl.BlockSpec((octants, width, width), lambda g: (chunk, 0, 0)),
        ]
        operands += [high, low, transfer]
    flops = 2 * classes * tile * width * (rows + width)
    return pl.pallas_call(
        functools.partial(translate_kernel, spread is not None, devices),
        grid=(1,),
        in_specs=in_specs,
        out_specs=pl.BlockSpec((tile, width), lambda g: (0, 0)),
        out_shape=jax.ShapeDtypeStruct((tile, width), jnp.float32),
        scratch_shapes=[pltpu.VMEM((slot.shape[0], tile, 1), jnp.int32)],
        compiler_params=pltpu.CompilerParams(vmem_limit_bytes=48 * 1024 * 1024),
        cost_estimate=pl.CostEstimate(
            flops=flops, bytes_accessed=2 * kernels.size + 2 * buffer.size, transcendentals=0
        ),
    )(*operands)


def on_device(
    multipoles,
    kernels,
    transfer,
    leaf_target,
    leaf_source,
    leaf_count,
    coarse_target,
    coarse_source,
    coarse_count,
    ghost_send,
    coarse_send,
):
    width = multipoles.shape[1]
    rounds = lax.axis_size("leaf").bit_length() - 1
    boxes = multipoles.shape[0]
    parents = boxes // 8
    classes = kernels.shape[0]
    leaf_ghost = ghost_send.shape[2]
    coarse_ghost = coarse_send.shape[2]
    leaf_rows = boxes + rounds * leaf_ghost
    coarse_rows = parents + rounds * coarse_ghost

    child = 8 * lax.broadcasted_iota(jnp.int32, (16, parents), 1) + lax.broadcasted_iota(
        jnp.int32, (16, parents), 0
    )
    child = jnp.where(child % 8 == lax.broadcasted_iota(jnp.int32, (16, parents), 0), child, boxes)
    parent = translate(child, multipoles, transfer, 0, parents).astype(jnp.bfloat16)

    coarse_slot = slot_table(coarse_target[0], coarse_source[0], coarse_count[0], coarse_rows)
    chunks = 4
    devices = lax.axis_size("off")
    span = parents // devices
    per = 8 // chunks
    coarse_slot = jnp.pad(coarse_slot, ((0, 16 - classes), (0, 0)), constant_values=coarse_rows)

    leaf_region = -(-leaf_rows // coarse_rows) * coarse_rows
    rows_all = jnp.zeros((leaf_region + coarse_rows, width), multipoles.dtype)
    rows_all = lax.dynamic_update_slice(rows_all, multipoles, (0, 0))
    rows_all = lax.dynamic_update_slice(rows_all, parent, (leaf_region, 0))
    group = -(-classes // (rounds - 1))
    groups = [(low, min(low + group, classes)) for low in range(0, classes, group)]
    slot_parts = []
    for bit_index in range(rounds):
        picks = jnp.concatenate([ghost_send[0, bit_index], coarse_send[0, bit_index] + leaf_region])
        outgoing = rows_all[picks]
        if bit_index < len(groups):
            low, high = groups[bit_index]
            tables, outgoing = lax.optimization_barrier(
                ((leaf_target[0, low:high], leaf_source[0, low:high], leaf_count[0, low:high]), outgoing)
            )
        arrived = partner(outgoing, "leaf", bit_index)
        if bit_index < len(groups):
            part, arrived = lax.optimization_barrier((slot_table(*tables, leaf_rows), arrived))
            slot_parts.append(part)
        rows_all = lax.dynamic_update_slice(
            rows_all, arrived[:leaf_ghost], (boxes + bit_index * leaf_ghost, 0)
        )
        rows_all = lax.dynamic_update_slice(
            rows_all, arrived[leaf_ghost:], (leaf_region + parents + bit_index * coarse_ghost, 0)
        )

    leaf_slot = jnp.concatenate(slot_parts, axis=0)
    leaf_slot = leaf_slot.reshape(classes, devices, span, chunks, per)
    leaf_slot = leaf_slot.transpose(0, 3, 1, 4, 2).reshape(classes, boxes)
    leaf_slot = jnp.pad(leaf_slot, ((0, 16 - classes), (0, 0)), constant_values=leaf_rows)
    coarse_local = 0.5 * translate(coarse_slot, rows_all[leaf_region:], kernels, 0, parents)
    coarse_high = coarse_local.astype(jnp.bfloat16)
    coarse_low = (coarse_local - coarse_high.astype(jnp.float32)).astype(jnp.bfloat16)
    tile = boxes // chunks
    block = tile // devices
    me = lax.axis_index("off")
    mine = []
    for chunk in range(chunks):
        slot_in = leaf_slot
        if chunk >= 2:
            slot_in, _ = lax.optimization_barrier((leaf_slot, mine[chunk - 2]))
        partial_sum = translate(
            slot_in, rows_all, kernels, chunk, tile, (coarse_high, coarse_low, transfer), devices,
            rows=leaf_rows,
        )
        total = lax.dynamic_slice_in_dim(partial_sum, me * block, block, 0)
        for shift in range(1, devices):
            theirs = lax.rem(me + shift, devices)
            sent = lax.dynamic_slice_in_dim(partial_sum, theirs * block, block, 0)
            route = [(k, (k + shift) % devices) for k in range(devices)]
            total = total + lax.ppermute(sent, "off", route)
        mine.append(total)
    mine = jnp.stack(mine).reshape(8, span, width)
    return mine.transpose(1, 0, 2).reshape(-1, width)


def solution(mesh):
    in_specs = (
        P("leaf", None),
        P("off", None, None),
        P(),
        P("leaf", "off", None),
        P("leaf", "off", None),
        P("leaf", "off"),
        P("leaf", "off", None),
        P("leaf", "off", None),
        P("leaf", "off"),
        P("leaf", None, None),
        P("leaf", None, None),
    )
    out_specs = P(("leaf", "off"), None)
    return jax.shard_map(
        on_device, mesh=mesh, in_specs=in_specs, out_specs=out_specs, check_vma=False
    )
```

```python
import functools

import jax
import jax.numpy as jnp
from jax import lax
from jax.experimental import pallas as pl
from jax.experimental.pallas import tpu as pltpu
from jax.sharding import PartitionSpec as P


def partner(block, axis, apart):
    count = lax.axis_size(axis)
    route = []
    for low in range(count):
        high = low | 1 << apart
        if high != low and high < count:
            route += [(low, high), (high, low)]
    return lax.ppermute(block, axis, route)


def invert_kernel(target_ref, payload_ref, out_ref):
    pairs = target_ref.shape[1]
    columns = jnp.transpose(target_ref[...])
    spots = lax.broadcasted_iota(jnp.int32, (pairs, pairs), 1)
    for c in range(payload_ref.shape[0]):
        hot = (columns[:, c:c + 1] == spots).astype(payload_ref.dtype)
        parts = jnp.dot(payload_ref[c], hot, preferred_element_type=jnp.float32)
        out_ref[c:c + 1, :] = (parts[0:1] * 64.0 + parts[1:2]).astype(jnp.int32)


def slot_table(target, source, pair_count, pad_row):
    classes, pairs = target.shape
    pair = lax.broadcasted_iota(jnp.int32, target.shape, 1)
    payload = jnp.where(pair < pair_count[:, None], source, pad_row)
    split = jnp.stack([payload // 64, payload % 64], axis=1).astype(jnp.bfloat16)
    split = jnp.pad(split, ((0, 0), (0, 6), (0, 0)))
    target = jnp.pad(target, ((0, 16 - classes), (0, 0)), constant_values=-1)
    return pl.pallas_call(
        invert_kernel,
        out_shape=jax.ShapeDtypeStruct((classes, pairs), jnp.int32),
        compiler_params=pltpu.CompilerParams(vmem_limit_bytes=48 * 1024 * 1024),
        cost_estimate=pl.CostEstimate(
            flops=2 * 8 * classes * pairs * pairs, bytes_accessed=24 * classes * pairs, transcendentals=0
        ),
    )(target, split)


def translate_kernel(spread, devices, classes, slot_ref, buf_ref, k_ref, *rest):
    *rest, column_ref = rest
    step = pl.program_id(0)
    out_ref = rest[-1]

    def init(rest):
        if spread:
            high_ref, low_ref, t_ref, out_ref = rest
            nt = (((1,), (1,)), ((), ()))
            octants = t_ref.shape[0]
            span = high_ref.shape[0] // devices
            for h in range(octants):
                term = lax.dot_general(
                    high_ref[...], t_ref[h], nt, preferred_element_type=jnp.float32
                ) + lax.dot_general(low_ref[...], t_ref[h], nt, preferred_element_type=jnp.float32)
                for d in range(devices):
                    at = (d * octants + h) * span
                    out_ref[at:at + span, :] = term[d * span:(d + 1) * span]
        else:
            (out_ref,) = rest
            out_ref[...] = jnp.zeros(out_ref.shape, out_ref.dtype)

    @pl.when(step == 0)
    def _():
        init(rest)
        columns = jnp.transpose(slot_ref[...])
        for c in range(classes):
            column_ref[c] = columns[:, c:c + 1]

    rows = buf_ref.shape[0]
    tile = out_ref.shape[0]
    per_step = k_ref.shape[0]

    def one_class(c, carry):
        spots = lax.broadcasted_iota(jnp.int32, (tile, rows), 1)
        hot = (column_ref[step * per_step + c] == spots).astype(buf_ref.dtype)
        picked = jnp.dot(hot, buf_ref[...], preferred_element_type=jnp.float32)
        out_ref[...] += jnp.dot(
            picked.astype(k_ref.dtype), k_ref[c], preferred_element_type=jnp.float32
        )
        return carry

    lax.fori_loop(0, per_step, one_class, 0, unroll=True)


def translate(slot, buffer, kernels, chunk, tile, spread=None, devices=1, rows=None, row_block=0):
    classes = kernels.shape[0]
    width = buffer.shape[1]
    rows = rows or buffer.shape[0]
    in_specs = [
        pl.BlockSpec((slot.shape[0], tile), lambda g: (0, chunk)),
        pl.BlockSpec((rows, width), lambda g: (row_block, 0)),
        pl.BlockSpec((classes // 2, width, width), lambda g: (g, 0, 0)),
    ]
    operands = [slot, buffer, kernels]
    if spread is not None:
        high, low, transfer = spread
        octants = tile // high.shape[0]
        in_specs += [
            pl.BlockSpec(high.shape, lambda g: (0, 0)),
            pl.BlockSpec(low.shape, lambda g: (0, 0)),
            pl.BlockSpec((octants, width, width), lambda g: (chunk, 0, 0)),
        ]
        operands += [high, low, transfer]
    flops = 2 * classes * tile * width * (rows + width)
    return pl.pallas_call(
        functools.partial(translate_kernel, spread is not None, devices, classes),
        grid=(2,),
        in_specs=in_specs,
        out_specs=pl.BlockSpec((tile, width), lambda g: (0, 0)),
        out_shape=jax.ShapeDtypeStruct((tile, width), jnp.float32),
        scratch_shapes=[pltpu.VMEM((slot.shape[0], tile, 1), jnp.int32)],
        compiler_params=pltpu.CompilerParams(vmem_limit_bytes=48 * 1024 * 1024),
        cost_estimate=pl.CostEstimate(
            flops=flops, bytes_accessed=2 * kernels.size + 2 * buffer.size, transcendentals=0
        ),
    )(*operands)


def on_device(
    multipoles,
    kernels,
    transfer,
    leaf_target,
    leaf_source,
    leaf_count,
    coarse_target,
    coarse_source,
    coarse_count,
    ghost_send,
    coarse_send,
):
    width = multipoles.shape[1]
    rounds = lax.axis_size("leaf").bit_length() - 1
    boxes = multipoles.shape[0]
    parents = boxes // 8
    classes = kernels.shape[0]
    leaf_ghost = ghost_send.shape[2]
    coarse_ghost = coarse_send.shape[2]
    leaf_rows = boxes + rounds * leaf_ghost
    coarse_rows = parents + rounds * coarse_ghost

    child = 8 * lax.broadcasted_iota(jnp.int32, (16, parents), 1) + lax.broadcasted_iota(
        jnp.int32, (16, parents), 0
    )
    child = jnp.where(child % 8 == lax.broadcasted_iota(jnp.int32, (16, parents), 0), child, boxes)
    parent = translate(child, multipoles, transfer, 0, parents).astype(jnp.bfloat16)

    coarse_slot = slot_table(coarse_target[0], coarse_source[0], coarse_count[0], coarse_rows)
    chunks = 4
    devices = lax.axis_size("off")
    span = parents // devices
    per = 8 // chunks
    coarse_slot = jnp.pad(coarse_slot, ((0, 16 - classes), (0, 0)), constant_values=coarse_rows)

    leaf_region = -(-leaf_rows // coarse_rows) * coarse_rows
    rows_all = jnp.zeros((leaf_region + coarse_rows, width), multipoles.dtype)
    rows_all = lax.dynamic_update_slice(rows_all, multipoles, (0, 0))
    rows_all = lax.dynamic_update_slice(rows_all, parent, (leaf_region, 0))
    group = -(-classes // (rounds - 1))
    groups = [(low, min(low + group, classes)) for low in range(0, classes, group)]
    slot_parts = []
    for bit_index in range(rounds):
        picks = jnp.concatenate([ghost_send[0, bit_index], coarse_send[0, bit_index] + leaf_region])
        outgoing = rows_all[picks]
        if bit_index < len(groups):
            low, high = groups[bit_index]
            tables, outgoing = lax.optimization_barrier(
                ((leaf_target[0, low:high], leaf_source[0, low:high], leaf_count[0, low:high]), outgoing)
            )
        arrived = partner(outgoing, "leaf", bit_index)
        if bit_index < len(groups):
            part, arrived = lax.optimization_barrier((slot_table(*tables, leaf_rows), arrived))
            slot_parts.append(part)
        rows_all = lax.dynamic_update_slice(
            rows_all, arrived[:leaf_ghost], (boxes + bit_index * leaf_ghost, 0)
        )
        rows_all = lax.dynamic_update_slice(
            rows_all, arrived[leaf_ghost:], (leaf_region + parents + bit_index * coarse_ghost, 0)
        )

    leaf_slot = jnp.concatenate(slot_parts, axis=0)
    leaf_slot = leaf_slot.reshape(classes, devices, span, chunks, per)
    leaf_slot = leaf_slot.transpose(0, 3, 1, 4, 2).reshape(classes, boxes)
    leaf_slot = jnp.pad(leaf_slot, ((0, 16 - classes), (0, 0)), constant_values=leaf_rows)
    coarse_local = 0.5 * translate(
        coarse_slot, rows_all, kernels, 0, parents, rows=coarse_rows, row_block=leaf_region // coarse_rows
    )
    coarse_high = coarse_local.astype(jnp.bfloat16)
    coarse_low = (coarse_local - coarse_high.astype(jnp.float32)).astype(jnp.bfloat16)
    tile = boxes // chunks
    block = tile // devices
    me = lax.axis_index("off")
    mine = []
    for chunk in range(chunks):
        slot_in = leaf_slot
        if chunk >= 2:
            slot_in, _ = lax.optimization_barrier((leaf_slot, mine[chunk - 2]))
        partial_sum = translate(
            slot_in, rows_all, kernels, chunk, tile, (coarse_high, coarse_low, transfer), devices,
            rows=leaf_rows,
        )
        total = lax.dynamic_slice_in_dim(partial_sum, me * block, block, 0)
        for shift in range(1, devices):
            theirs = lax.rem(me + shift, devices)
            sent = lax.dynamic_slice_in_dim(partial_sum, theirs * block, block, 0)
            route = [(k, (k + shift) % devices) for k in range(devices)]
            total = total + lax.ppermute(sent, "off", route)
        mine.append(total)
    mine = jnp.stack(mine).reshape(8, span, width)
    return mine.transpose(1, 0, 2).reshape(-1, width)


def solution(mesh):
    in_specs = (
        P("leaf", None),
        P("off", None, None),
        P(),
        P("leaf", "off", None),
        P("leaf", "off", None),
        P("leaf", "off"),
        P("leaf", "off", None),
        P("leaf", "off", None),
        P("leaf", "off"),
        P("leaf", None, None),
        P("leaf", None, None),
    )
    out_specs = P(("leaf", "off"), None)
    return jax.shard_map(
        on_device, mesh=mesh, in_specs=in_specs, out_specs=out_specs, check_vma=False
    )
```

```python
import functools

import jax
import jax.numpy as jnp
from jax import lax
from jax.experimental import pallas as pl
from jax.experimental.pallas import tpu as pltpu
from jax.sharding import PartitionSpec as P


def partner(block, axis, apart):
    count = lax.axis_size(axis)
    route = []
    for low in range(count):
        high = low | 1 << apart
        if high != low and high < count:
            route += [(low, high), (high, low)]
    return lax.ppermute(block, axis, route)


def invert_kernel(target_ref, payload_ref, out_ref):
    pairs = target_ref.shape[1]
    columns = jnp.transpose(target_ref[...])
    spots = lax.broadcasted_iota(jnp.int32, (pairs, pairs), 1)
    for c in range(payload_ref.shape[0]):
        hot = (columns[:, c:c + 1] == spots).astype(payload_ref.dtype)
        parts = jnp.dot(payload_ref[c], hot, preferred_element_type=jnp.float32)
        out_ref[c:c + 1, :] = (parts[0:1] * 64.0 + parts[1:2]).astype(jnp.int32)


def slot_table(target, source, pair_count, pad_row):
    classes, pairs = target.shape
    pair = lax.broadcasted_iota(jnp.int32, target.shape, 1)
    payload = jnp.where(pair < pair_count[:, None], source, pad_row)
    split = jnp.stack([payload // 64, payload % 64], axis=1).astype(jnp.bfloat16)
    split = jnp.pad(split, ((0, 0), (0, 6), (0, 0)))
    target = jnp.pad(target, ((0, 16 - classes), (0, 0)), constant_values=-1)
    return pl.pallas_call(
        invert_kernel,
        out_shape=jax.ShapeDtypeStruct((classes, pairs), jnp.int32),
        compiler_params=pltpu.CompilerParams(vmem_limit_bytes=48 * 1024 * 1024),
        cost_estimate=pl.CostEstimate(
            flops=2 * 8 * classes * pairs * pairs, bytes_accessed=24 * classes * pairs, transcendentals=0
        ),
    )(target, split)


def translate_kernel(spread, devices, classes, slot_ref, buf_ref, k_ref, *rest):
    *rest, column_ref = rest
    step = pl.program_id(0)
    out_ref = rest[-1]

    def init(rest):
        if spread:
            high_ref, low_ref, t_ref, out_ref = rest
            nt = (((1,), (1,)), ((), ()))
            octants = t_ref.shape[0]
            span = high_ref.shape[0] // devices
            for h in range(octants):
                term = lax.dot_general(
                    high_ref[...], t_ref[h], nt, preferred_element_type=jnp.float32
                ) + lax.dot_general(low_ref[...], t_ref[h], nt, preferred_element_type=jnp.float32)
                for d in range(devices):
                    at = (d * octants + h) * span
                    out_ref[at:at + span, :] = term[d * span:(d + 1) * span]
        else:
            (out_ref,) = rest
            out_ref[...] = jnp.zeros(out_ref.shape, out_ref.dtype)

    @pl.when(step == 0)
    def _():
        init(rest)
        columns = jnp.transpose(slot_ref[...])
        for c in range(classes):
            column_ref[c] = columns[:, c:c + 1]

    rows = buf_ref.shape[0]
    tile = out_ref.shape[0]
    per_step = k_ref.shape[0]

    def one_class(c, carry):
        spots = lax.broadcasted_iota(jnp.int32, (tile, rows), 1)
        hot = (column_ref[step * per_step + c] == spots).astype(buf_ref.dtype)
        picked = jnp.dot(hot, buf_ref[...], preferred_element_type=jnp.float32)
        out_ref[...] += jnp.dot(
            picked.astype(k_ref.dtype), k_ref[c], preferred_element_type=jnp.float32
        )
        return carry

    lax.fori_loop(0, per_step, one_class, 0, unroll=True)


def translate(slot, buffer, kernels, chunk, tile, spread=None, devices=1, rows=None, row_block=0):
    classes = kernels.shape[0]
    width = buffer.shape[1]
    rows = rows or buffer.shape[0]
    in_specs = [
        pl.BlockSpec((slot.shape[0], tile), lambda g: (0, chunk)),
        pl.BlockSpec((rows, width), lambda g: (row_block, 0)),
        pl.BlockSpec((2, width, width), lambda g: (g, 0, 0)),
    ]
    operands = [slot, buffer, kernels]
    if spread is not None:
        high, low, transfer = spread
        octants = tile // high.shape[0]
        in_specs += [
            pl.BlockSpec(high.shape, lambda g: (0, 0)),
            pl.BlockSpec(low.shape, lambda g: (0, 0)),
            pl.BlockSpec((octants, width, width), lambda g: (chunk, 0, 0)),
        ]
        operands += [high, low, transfer]
    flops = 2 * classes * tile * width * (rows + width)
    return pl.pallas_call(
        functools.partial(translate_kernel, spread is not None, devices, classes),
        grid=(classes // 2,),
        in_specs=in_specs,
        out_specs=pl.BlockSpec((tile, width), lambda g: (0, 0)),
        out_shape=jax.ShapeDtypeStruct((tile, width), jnp.float32),
        scratch_shapes=[pltpu.VMEM((slot.shape[0], tile, 1), jnp.int32)],
        compiler_params=pltpu.CompilerParams(vmem_limit_bytes=48 * 1024 * 1024),
        cost_estimate=pl.CostEstimate(
            flops=flops, bytes_accessed=2 * kernels.size + 2 * buffer.size, transcendentals=0
        ),
    )(*operands)


def on_device(
    multipoles,
    kernels,
    transfer,
    leaf_target,
    leaf_source,
    leaf_count,
    coarse_target,
    coarse_source,
    coarse_count,
    ghost_send,
    coarse_send,
):
    width = multipoles.shape[1]
    rounds = lax.axis_size("leaf").bit_length() - 1
    boxes = multipoles.shape[0]
    parents = boxes // 8
    classes = kernels.shape[0]
    leaf_ghost = ghost_send.shape[2]
    coarse_ghost = coarse_send.shape[2]
    leaf_rows = boxes + rounds * leaf_ghost
    coarse_rows = parents + rounds * coarse_ghost

    child = 8 * lax.broadcasted_iota(jnp.int32, (16, parents), 1) + lax.broadcasted_iota(
        jnp.int32, (16, parents), 0
    )
    child = jnp.where(child % 8 == lax.broadcasted_iota(jnp.int32, (16, parents), 0), child, boxes)
    parent = translate(child, multipoles, transfer, 0, parents).astype(jnp.bfloat16)

    coarse_slot = slot_table(coarse_target[0], coarse_source[0], coarse_count[0], coarse_rows)
    chunks = 4
    devices = lax.axis_size("off")
    span = parents // devices
    per = 8 // chunks
    coarse_slot = jnp.pad(coarse_slot, ((0, 16 - classes), (0, 0)), constant_values=coarse_rows)

    leaf_region = -(-leaf_rows // coarse_rows) * coarse_rows
    rows_all = jnp.zeros((leaf_region + coarse_rows, width), multipoles.dtype)
    rows_all = lax.dynamic_update_slice(rows_all, multipoles, (0, 0))
    rows_all = lax.dynamic_update_slice(rows_all, parent, (leaf_region, 0))
    group = -(-classes // (rounds - 1))
    groups = [(low, min(low + group, classes)) for low in range(0, classes, group)]
    slot_parts = []
    for bit_index in range(rounds):
        picks = jnp.concatenate([ghost_send[0, bit_index], coarse_send[0, bit_index] + leaf_region])
        outgoing = rows_all[picks]
        if bit_index < len(groups):
            low, high = groups[bit_index]
            tables, outgoing = lax.optimization_barrier(
                ((leaf_target[0, low:high], leaf_source[0, low:high], leaf_count[0, low:high]), outgoing)
            )
        arrived = partner(outgoing, "leaf", bit_index)
        if bit_index < len(groups):
            part, arrived = lax.optimization_barrier((slot_table(*tables, leaf_rows), arrived))
            slot_parts.append(part)
        rows_all = lax.dynamic_update_slice(
            rows_all, arrived[:leaf_ghost], (boxes + bit_index * leaf_ghost, 0)
        )
        rows_all = lax.dynamic_update_slice(
            rows_all, arrived[leaf_ghost:], (leaf_region + parents + bit_index * coarse_ghost, 0)
        )

    leaf_slot = jnp.concatenate(slot_parts, axis=0)
    leaf_slot = leaf_slot.reshape(classes, devices, span, chunks, per)
    leaf_slot = leaf_slot.transpose(0, 3, 1, 4, 2).reshape(classes, boxes)
    leaf_slot = jnp.pad(leaf_slot, ((0, 16 - classes), (0, 0)), constant_values=leaf_rows)
    coarse_local = 0.5 * translate(
        coarse_slot, rows_all, kernels, 0, parents, rows=coarse_rows, row_block=leaf_region // coarse_rows
    )
    coarse_high = coarse_local.astype(jnp.bfloat16)
    coarse_low = (coarse_local - coarse_high.astype(jnp.float32)).astype(jnp.bfloat16)
    tile = boxes // chunks
    block = tile // devices
    me = lax.axis_index("off")
    mine = []
    for chunk in range(chunks):
        slot_in = leaf_slot
        if chunk >= 2:
            slot_in, _ = lax.optimization_barrier((leaf_slot, mine[chunk - 2]))
        partial_sum = translate(
            slot_in, rows_all, kernels, chunk, tile, (coarse_high, coarse_low, transfer), devices,
            rows=leaf_rows,
        )
        total = lax.dynamic_slice_in_dim(partial_sum, me * block, block, 0)
        for shift in range(1, devices):
            theirs = lax.rem(me + shift, devices)
            sent = lax.dynamic_slice_in_dim(partial_sum, theirs * block, block, 0)
            route = [(k, (k + shift) % devices) for k in range(devices)]
            total = total + lax.ppermute(sent, "off", route)
        mine.append(total)
    mine = jnp.stack(mine).reshape(8, span, width)
    return mine.transpose(1, 0, 2).reshape(-1, width)


def solution(mesh):
    in_specs = (
        P("leaf", None),
        P("off", None, None),
        P(),
        P("leaf", "off", None),
        P("leaf", "off", None),
        P("leaf", "off"),
        P("leaf", "off", None),
        P("leaf", "off", None),
        P("leaf", "off"),
        P("leaf", None, None),
        P("leaf", None, None),
    )
    out_specs = P(("leaf", "off"), None)
    return jax.shard_map(
        on_device, mesh=mesh, in_specs=in_specs, out_specs=out_specs, check_vma=False
    )
```

```python
import functools

import jax
import jax.numpy as jnp
from jax import lax
from jax.experimental import pallas as pl
from jax.experimental.pallas import tpu as pltpu
from jax.sharding import PartitionSpec as P


def partner(block, axis, apart):
    count = lax.axis_size(axis)
    route = []
    for low in range(count):
        high = low | 1 << apart
        if high != low and high < count:
            route += [(low, high), (high, low)]
    return lax.ppermute(block, axis, route)


def invert_kernel(target_ref, payload_ref, out_ref):
    pairs = target_ref.shape[1]
    columns = jnp.transpose(target_ref[...])
    spots = lax.broadcasted_iota(jnp.int32, (pairs, pairs), 1)
    for c in range(payload_ref.shape[0]):
        hot = (columns[:, c:c + 1] == spots).astype(payload_ref.dtype)
        parts = jnp.dot(payload_ref[c], hot, preferred_element_type=jnp.float32)
        out_ref[c:c + 1, :] = (parts[0:1] * 64.0 + parts[1:2]).astype(jnp.int32)


def slot_table(target, source, pair_count, pad_row):
    classes, pairs = target.shape
    pair = lax.broadcasted_iota(jnp.int32, target.shape, 1)
    payload = jnp.where(pair < pair_count[:, None], source, pad_row)
    split = jnp.stack([payload // 64, payload % 64], axis=1).astype(jnp.bfloat16)
    split = jnp.pad(split, ((0, 0), (0, 6), (0, 0)))
    target = jnp.pad(target, ((0, 16 - classes), (0, 0)), constant_values=-1)
    return pl.pallas_call(
        invert_kernel,
        out_shape=jax.ShapeDtypeStruct((classes, pairs), jnp.int32),
        compiler_params=pltpu.CompilerParams(vmem_limit_bytes=48 * 1024 * 1024),
        cost_estimate=pl.CostEstimate(
            flops=2 * 8 * classes * pairs * pairs, bytes_accessed=24 * classes * pairs, transcendentals=0
        ),
    )(target, split)


def translate_kernel(spread, devices, classes, slot_ref, buf_ref, k_ref, *rest):
    *rest, column_ref = rest
    step = pl.program_id(0)
    out_ref = rest[-1]

    def init(rest):
        if spread:
            high_ref, low_ref, t_ref, out_ref = rest
            nt = (((1,), (1,)), ((), ()))
            octants = t_ref.shape[0]
            span = high_ref.shape[0] // devices
            for h in range(octants):
                term = lax.dot_general(
                    high_ref[...], t_ref[h], nt, preferred_element_type=jnp.float32
                ) + lax.dot_general(low_ref[...], t_ref[h], nt, preferred_element_type=jnp.float32)
                for d in range(devices):
                    at = (d * octants + h) * span
                    out_ref[at:at + span, :] = term[d * span:(d + 1) * span]
        else:
            (out_ref,) = rest
            out_ref[...] = jnp.zeros(out_ref.shape, out_ref.dtype)

    @pl.when(step == 0)
    def _():
        init(rest)
        columns = jnp.transpose(slot_ref[...])
        for c in range(classes):
            column_ref[c] = columns[:, c:c + 1]

    rows = buf_ref.shape[0]
    tile = out_ref.shape[0]
    per_step = k_ref.shape[0]

    def one_class(c, carry):
        spots = lax.broadcasted_iota(jnp.int32, (tile, rows), 1)
        hot = (column_ref[step * per_step + c] == spots).astype(buf_ref.dtype)
        picked = jnp.dot(hot, buf_ref[...], preferred_element_type=jnp.float32)
        out_ref[...] += jnp.dot(
            picked.astype(k_ref.dtype), k_ref[c], preferred_element_type=jnp.float32
        )
        return carry

    lax.fori_loop(0, per_step, one_class, 0, unroll=True)


def translate(slot, buffer, kernels, chunk, tile, spread=None, devices=1, rows=None, row_block=0):
    classes = kernels.shape[0]
    width = buffer.shape[1]
    rows = rows or buffer.shape[0]
    in_specs = [
        pl.BlockSpec((slot.shape[0], tile), lambda g: (0, chunk)),
        pl.BlockSpec((rows, width), lambda g: (row_block, 0)),
        pl.BlockSpec((classes // 2, width, width), lambda g: (g, 0, 0)),
    ]
    operands = [slot, buffer, kernels]
    if spread is not None:
        high, low, transfer = spread
        octants = tile // high.shape[0]
        in_specs += [
            pl.BlockSpec(high.shape, lambda g: (0, 0)),
            pl.BlockSpec(low.shape, lambda g: (0, 0)),
            pl.BlockSpec((octants, width, width), lambda g: (chunk, 0, 0)),
        ]
        operands += [high, low, transfer]
    flops = 2 * classes * tile * width * (rows + width)
    return pl.pallas_call(
        functools.partial(translate_kernel, spread is not None, devices, classes),
        grid=(2,),
        in_specs=in_specs,
        out_specs=pl.BlockSpec((tile, width), lambda g: (0, 0)),
        out_shape=jax.ShapeDtypeStruct((tile, width), jnp.float32),
        scratch_shapes=[pltpu.VMEM((slot.shape[0], tile, 1), jnp.int32)],
        compiler_params=pltpu.CompilerParams(vmem_limit_bytes=48 * 1024 * 1024),
        cost_estimate=pl.CostEstimate(
            flops=flops, bytes_accessed=2 * kernels.size + 2 * buffer.size, transcendentals=0
        ),
    )(*operands)


def first_kernel(devices, classes, slot_ref, buf_ref, k_ref, cslot_ref, cbuf_ref, t_ref,
                 out_ref, high_ref, low_ref, column_ref, ccolumn_ref, cacc_ref):
    step = pl.program_id(0)
    per_step = k_ref.shape[0]

    @pl.when(step == 0)
    def _():
        out_ref[...] = jnp.zeros(out_ref.shape, out_ref.dtype)
        cacc_ref[...] = jnp.zeros(cacc_ref.shape, cacc_ref.dtype)
        columns = jnp.transpose(slot_ref[...])
        ccolumns = jnp.transpose(cslot_ref[...])
        for c in range(classes):
            column_ref[c] = columns[:, c:c + 1]
            ccolumn_ref[c] = ccolumns[:, c:c + 1]

    def one_class(c, carry):
        k = k_ref[c]
        spots = lax.broadcasted_iota(jnp.int32, (out_ref.shape[0], buf_ref.shape[0]), 1)
        hot = (column_ref[step * per_step + c] == spots).astype(buf_ref.dtype)
        picked = jnp.dot(hot, buf_ref[...], preferred_element_type=jnp.float32)
        out_ref[...] += jnp.dot(picked.astype(k.dtype), k, preferred_element_type=jnp.float32)
        cspots = lax.broadcasted_iota(jnp.int32, (cacc_ref.shape[0], cbuf_ref.shape[0]), 1)
        chot = (ccolumn_ref[step * per_step + c] == cspots).astype(cbuf_ref.dtype)
        cpicked = jnp.dot(chot, cbuf_ref[...], preferred_element_type=jnp.float32)
        cacc_ref[...] += jnp.dot(cpicked.astype(k.dtype), k, preferred_element_type=jnp.float32)
        return carry

    lax.fori_loop(0, per_step, one_class, 0, unroll=True)

    @pl.when(step == pl.num_programs(0) - 1)
    def _():
        local = 0.5 * cacc_ref[...]
        high = local.astype(high_ref.dtype)
        low = (local - high.astype(jnp.float32)).astype(low_ref.dtype)
        high_ref[...] = high
        low_ref[...] = low
        nt = (((1,), (1,)), ((), ()))
        octants = t_ref.shape[0]
        span = high.shape[0] // devices
        for h in range(octants):
            term = lax.dot_general(
                high, t_ref[h], nt, preferred_element_type=jnp.float32
            ) + lax.dot_general(low, t_ref[h], nt, preferred_element_type=jnp.float32)
            for d in range(devices):
                at = (d * octants + h) * span
                out_ref[at:at + span, :] += term[d * span:(d + 1) * span]


def first_chunk(slot, rows_all, leaf_rows, kernels, coarse_slot, coarse_rows, transfer, tile, devices):
    classes = kernels.shape[0]
    width = rows_all.shape[1]
    parents = coarse_slot.shape[1]
    octants = tile // parents
    return pl.pallas_call(
        functools.partial(first_kernel, devices, classes),
        grid=(2,),
        in_specs=[
            pl.BlockSpec((slot.shape[0], tile), lambda g: (0, 0)),
            pl.BlockSpec((leaf_rows, width), lambda g: (0, 0)),
            pl.BlockSpec((classes // 2, width, width), lambda g: (g, 0, 0)),
            pl.BlockSpec(coarse_slot.shape, lambda g: (0, 0)),
            pl.BlockSpec(coarse_rows.shape, lambda g: (0, 0)),
            pl.BlockSpec((octants, width, width), lambda g: (0, 0, 0)),
        ],
        out_specs=[
            pl.BlockSpec((tile, width), lambda g: (0, 0)),
            pl.BlockSpec((parents, width), lambda g: (0, 0)),
            pl.BlockSpec((parents, width), lambda g: (0, 0)),
        ],
        out_shape=[
            jax.ShapeDtypeStruct((tile, width), jnp.float32),
            jax.ShapeDtypeStruct((parents, width), jnp.bfloat16),
            jax.ShapeDtypeStruct((parents, width), jnp.bfloat16),
        ],
        scratch_shapes=[
            pltpu.VMEM((slot.shape[0], tile, 1), jnp.int32),
            pltpu.VMEM((coarse_slot.shape[0], parents, 1), jnp.int32),
            pltpu.VMEM((parents, width), jnp.float32),
        ],
        compiler_params=pltpu.CompilerParams(vmem_limit_bytes=48 * 1024 * 1024),
        cost_estimate=pl.CostEstimate(
            flops=2 * classes * tile * width * (leaf_rows + width), bytes_accessed=2 * kernels.size,
            transcendentals=0,
        ),
    )(slot, rows_all, kernels, coarse_slot, coarse_rows, transfer)


def on_device(
    multipoles,
    kernels,
    transfer,
    leaf_target,
    leaf_source,
    leaf_count,
    coarse_target,
    coarse_source,
    coarse_count,
    ghost_send,
    coarse_send,
):
    width = multipoles.shape[1]
    rounds = lax.axis_size("leaf").bit_length() - 1
    boxes = multipoles.shape[0]
    parents = boxes // 8
    classes = kernels.shape[0]
    leaf_ghost = ghost_send.shape[2]
    coarse_ghost = coarse_send.shape[2]
    leaf_rows = boxes + rounds * leaf_ghost
    coarse_rows = parents + rounds * coarse_ghost

    child = 8 * lax.broadcasted_iota(jnp.int32, (16, parents), 1) + lax.broadcasted_iota(
        jnp.int32, (16, parents), 0
    )
    child = jnp.where(child % 8 == lax.broadcasted_iota(jnp.int32, (16, parents), 0), child, boxes)
    parent = translate(child, multipoles, transfer, 0, parents).astype(jnp.bfloat16)

    coarse_slot = slot_table(coarse_target[0], coarse_source[0], coarse_count[0], coarse_rows)
    chunks = 4
    devices = lax.axis_size("off")
    span = parents // devices
    per = 8 // chunks
    coarse_slot = jnp.pad(coarse_slot, ((0, 16 - classes), (0, 0)), constant_values=coarse_rows)

    leaf_region = -(-leaf_rows // coarse_rows) * coarse_rows
    rows_all = jnp.zeros((leaf_region + coarse_rows, width), multipoles.dtype)
    rows_all = lax.dynamic_update_slice(rows_all, multipoles, (0, 0))
    rows_all = lax.dynamic_update_slice(rows_all, parent, (leaf_region, 0))
    group = -(-classes // (rounds - 1))
    groups = [(low, min(low + group, classes)) for low in range(0, classes, group)]
    slot_parts = []
    for bit_index in range(rounds):
        picks = jnp.concatenate([ghost_send[0, bit_index], coarse_send[0, bit_index] + leaf_region])
        outgoing = rows_all[picks]
        if bit_index < len(groups):
            low, high = groups[bit_index]
            tables, outgoing = lax.optimization_barrier(
                ((leaf_target[0, low:high], leaf_source[0, low:high], leaf_count[0, low:high]), outgoing)
            )
        arrived = partner(outgoing, "leaf", bit_index)
        if bit_index < len(groups):
            part, arrived = lax.optimization_barrier((slot_table(*tables, leaf_rows), arrived))
            slot_parts.append(part)
        rows_all = lax.dynamic_update_slice(
            rows_all, arrived[:leaf_ghost], (boxes + bit_index * leaf_ghost, 0)
        )
        rows_all = lax.dynamic_update_slice(
            rows_all, arrived[leaf_ghost:], (leaf_region + parents + bit_index * coarse_ghost, 0)
        )

    leaf_slot = jnp.concatenate(slot_parts, axis=0)
    leaf_slot = leaf_slot.reshape(classes, devices, span, chunks, per)
    leaf_slot = leaf_slot.transpose(0, 3, 1, 4, 2).reshape(classes, boxes)
    leaf_slot = jnp.pad(leaf_slot, ((0, 16 - classes), (0, 0)), constant_values=leaf_rows)
    tile = boxes // chunks
    block = tile // devices
    me = lax.axis_index("off")
    mine = []
    for chunk in range(chunks):
        slot_in = leaf_slot
        if chunk >= 2:
            slot_in, _ = lax.optimization_barrier((leaf_slot, mine[chunk - 2]))
        if chunk == 0:
            partial_sum, coarse_high, coarse_low = first_chunk(
                slot_in, rows_all, leaf_rows, kernels, coarse_slot, rows_all[leaf_region:],
                transfer, tile, devices,
            )
        else:
            partial_sum = translate(
                slot_in, rows_all, kernels, chunk, tile, (coarse_high, coarse_low, transfer),
                devices, rows=leaf_rows,
            )
        total = lax.dynamic_slice_in_dim(partial_sum, me * block, block, 0)
        for shift in range(1, devices):
            theirs = lax.rem(me + shift, devices)
            sent = lax.dynamic_slice_in_dim(partial_sum, theirs * block, block, 0)
            route = [(k, (k + shift) % devices) for k in range(devices)]
            total = total + lax.ppermute(sent, "off", route)
        mine.append(total)
    mine = jnp.stack(mine).reshape(8, span, width)
    return mine.transpose(1, 0, 2).reshape(-1, width)


def solution(mesh):
    in_specs = (
        P("leaf", None),
        P("off", None, None),
        P(),
        P("leaf", "off", None),
        P("leaf", "off", None),
        P("leaf", "off"),
        P("leaf", "off", None),
        P("leaf", "off", None),
        P("leaf", "off"),
        P("leaf", None, None),
        P("leaf", None, None),
    )
    out_specs = P(("leaf", "off"), None)
    return jax.shard_map(
        on_device, mesh=mesh, in_specs=in_specs, out_specs=out_specs, check_vma=False
    )
```

```python
import functools

import jax
import jax.numpy as jnp
from jax import lax
from jax.experimental import pallas as pl
from jax.experimental.pallas import tpu as pltpu
from jax.sharding import PartitionSpec as P


def partner(block, axis, apart):
    count = lax.axis_size(axis)
    route = []
    for low in range(count):
        high = low | 1 << apart
        if high != low and high < count:
            route += [(low, high), (high, low)]
    return lax.ppermute(block, axis, route)


def invert_kernel(target_ref, payload_ref, out_ref):
    pairs = target_ref.shape[1]
    columns = jnp.transpose(target_ref[...])
    spots = lax.broadcasted_iota(jnp.int32, (pairs, pairs), 1)
    for c in range(payload_ref.shape[0]):
        hot = (columns[:, c:c + 1] == spots).astype(payload_ref.dtype)
        parts = jnp.dot(payload_ref[c], hot, preferred_element_type=jnp.float32)
        out_ref[c:c + 1, :] = (parts[0:1] * 64.0 + parts[1:2]).astype(jnp.int32)


def slot_table(target, source, pair_count, pad_row):
    classes, pairs = target.shape
    pair = lax.broadcasted_iota(jnp.int32, target.shape, 1)
    payload = jnp.where(pair < pair_count[:, None], source, pad_row)
    split = jnp.stack([payload // 64, payload % 64], axis=1).astype(jnp.bfloat16)
    split = jnp.pad(split, ((0, 0), (0, 6), (0, 0)))
    target = jnp.pad(target, ((0, 16 - classes), (0, 0)), constant_values=-1)
    return pl.pallas_call(
        invert_kernel,
        out_shape=jax.ShapeDtypeStruct((classes, pairs), jnp.int32),
        compiler_params=pltpu.CompilerParams(vmem_limit_bytes=48 * 1024 * 1024),
        cost_estimate=pl.CostEstimate(
            flops=2 * 8 * classes * pairs * pairs, bytes_accessed=24 * classes * pairs, transcendentals=0
        ),
    )(target, split)


def translate_kernel(spread, devices, classes, slot_ref, buf_ref, k_ref, *rest):
    *rest, column_ref = rest
    step = pl.program_id(0)
    out_ref = rest[-1]

    def init(rest):
        if spread:
            high_ref, low_ref, t_ref, out_ref = rest
            nt = (((1,), (1,)), ((), ()))
            octants = t_ref.shape[0]
            span = high_ref.shape[0] // devices
            for h in range(octants):
                term = lax.dot_general(
                    high_ref[...], t_ref[h], nt, preferred_element_type=jnp.float32
                ) + lax.dot_general(low_ref[...], t_ref[h], nt, preferred_element_type=jnp.float32)
                for d in range(devices):
                    at = (d * octants + h) * span
                    out_ref[at:at + span, :] = term[d * span:(d + 1) * span]
        else:
            (out_ref,) = rest
            out_ref[...] = jnp.zeros(out_ref.shape, out_ref.dtype)

    @pl.when(step == 0)
    def _():
        init(rest)
        columns = jnp.transpose(slot_ref[...])
        for c in range(classes):
            column_ref[c] = columns[:, c:c + 1]

    rows = buf_ref.shape[0]
    tile = out_ref.shape[0]
    per_step = k_ref.shape[0]

    def one_class(c, carry):
        spots = lax.broadcasted_iota(jnp.int32, (tile, rows), 1)
        hot = (column_ref[step * per_step + c] == spots).astype(buf_ref.dtype)
        picked = jnp.dot(hot, buf_ref[...], preferred_element_type=jnp.float32)
        out_ref[...] += jnp.dot(
            picked.astype(k_ref.dtype), k_ref[c], preferred_element_type=jnp.float32
        )
        return carry

    lax.fori_loop(0, per_step, one_class, 0, unroll=True)


def translate(slot, buffer, kernels, chunk, tile, spread=None, devices=1, rows=None, row_block=0):
    classes = kernels.shape[0]
    width = buffer.shape[1]
    rows = rows or buffer.shape[0]
    in_specs = [
        pl.BlockSpec((slot.shape[0], tile), lambda g: (0, chunk)),
        pl.BlockSpec((rows, width), lambda g: (row_block, 0)),
        pl.BlockSpec((classes // 2, width, width), lambda g: (g, 0, 0)),
    ]
    operands = [slot, buffer, kernels]
    if spread is not None:
        high, low, transfer = spread
        octants = tile // high.shape[0]
        in_specs += [
            pl.BlockSpec(high.shape, lambda g: (0, 0)),
            pl.BlockSpec(low.shape, lambda g: (0, 0)),
            pl.BlockSpec((octants, width, width), lambda g: (chunk, 0, 0)),
        ]
        operands += [high, low, transfer]
    flops = 2 * classes * tile * width * (rows + width)
    return pl.pallas_call(
        functools.partial(translate_kernel, spread is not None, devices, classes),
        grid=(2,),
        in_specs=in_specs,
        out_specs=pl.BlockSpec((tile, width), lambda g: (0, 0)),
        out_shape=jax.ShapeDtypeStruct((tile, width), jnp.float32),
        scratch_shapes=[pltpu.VMEM((slot.shape[0], tile, 1), jnp.int32)],
        compiler_params=pltpu.CompilerParams(vmem_limit_bytes=48 * 1024 * 1024),
        cost_estimate=pl.CostEstimate(
            flops=flops, bytes_accessed=2 * kernels.size + 2 * buffer.size, transcendentals=0
        ),
    )(*operands)


def first_kernel(devices, classes, slot_ref, buf_ref, k_ref, cslot_ref, cbuf_ref, t_ref,
                 out_ref, high_ref, low_ref, column_ref, ccolumn_ref, cacc_ref):
    step = pl.program_id(0)
    per_step = k_ref.shape[0]

    @pl.when(step == 0)
    def _():
        out_ref[...] = jnp.zeros(out_ref.shape, out_ref.dtype)
        cacc_ref[...] = jnp.zeros(cacc_ref.shape, cacc_ref.dtype)
        columns = jnp.transpose(slot_ref[...])
        ccolumns = jnp.transpose(cslot_ref[...])
        for c in range(classes):
            column_ref[c] = columns[:, c:c + 1]
            ccolumn_ref[c] = ccolumns[:, c:c + 1]

    def one_class(c, carry):
        k = k_ref[c]
        spots = lax.broadcasted_iota(jnp.int32, (out_ref.shape[0], buf_ref.shape[0]), 1)
        hot = (column_ref[step * per_step + c] == spots).astype(buf_ref.dtype)
        picked = jnp.dot(hot, buf_ref[...], preferred_element_type=jnp.float32)
        out_ref[...] += jnp.dot(picked.astype(k.dtype), k, preferred_element_type=jnp.float32)
        cspots = lax.broadcasted_iota(jnp.int32, (cacc_ref.shape[0], cbuf_ref.shape[0]), 1)
        chot = (ccolumn_ref[step * per_step + c] == cspots).astype(cbuf_ref.dtype)
        cpicked = jnp.dot(chot, cbuf_ref[...], preferred_element_type=jnp.float32)
        cacc_ref[...] += jnp.dot(cpicked.astype(k.dtype), k, preferred_element_type=jnp.float32)
        return carry

    lax.fori_loop(0, per_step, one_class, 0, unroll=True)

    @pl.when(step == pl.num_programs(0) - 1)
    def _():
        local = 0.5 * cacc_ref[...]
        high = local.astype(high_ref.dtype)
        low = (local - high.astype(jnp.float32)).astype(low_ref.dtype)
        high_ref[...] = high
        low_ref[...] = low
        nt = (((1,), (1,)), ((), ()))
        octants = t_ref.shape[0]
        span = high.shape[0] // devices
        for h in range(octants):
            term = lax.dot_general(
                high, t_ref[h], nt, preferred_element_type=jnp.float32
            ) + lax.dot_general(low, t_ref[h], nt, preferred_element_type=jnp.float32)
            for d in range(devices):
                at = (d * octants + h) * span
                out_ref[at:at + span, :] += term[d * span:(d + 1) * span]


def first_chunk(slot, rows_all, leaf_rows, kernels, coarse_slot, coarse_rows, transfer, tile, devices):
    classes = kernels.shape[0]
    width = rows_all.shape[1]
    parents = coarse_slot.shape[1]
    octants = tile // parents
    return pl.pallas_call(
        functools.partial(first_kernel, devices, classes),
        grid=(2,),
        in_specs=[
            pl.BlockSpec((slot.shape[0], tile), lambda g: (0, 0)),
            pl.BlockSpec((leaf_rows, width), lambda g: (0, 0)),
            pl.BlockSpec((classes // 2, width, width), lambda g: (g, 0, 0)),
            pl.BlockSpec(coarse_slot.shape, lambda g: (0, 0)),
            pl.BlockSpec(coarse_rows.shape, lambda g: (0, 0)),
            pl.BlockSpec((octants, width, width), lambda g: (0, 0, 0)),
        ],
        out_specs=[
            pl.BlockSpec((tile, width), lambda g: (0, 0)),
            pl.BlockSpec((parents, width), lambda g: (0, 0)),
            pl.BlockSpec((parents, width), lambda g: (0, 0)),
        ],
        out_shape=[
            jax.ShapeDtypeStruct((tile, width), jnp.float32),
            jax.ShapeDtypeStruct((parents, width), jnp.bfloat16),
            jax.ShapeDtypeStruct((parents, width), jnp.bfloat16),
        ],
        scratch_shapes=[
            pltpu.VMEM((slot.shape[0], tile, 1), jnp.int32),
            pltpu.VMEM((coarse_slot.shape[0], parents, 1), jnp.int32),
            pltpu.VMEM((parents, width), jnp.float32),
        ],
        compiler_params=pltpu.CompilerParams(vmem_limit_bytes=48 * 1024 * 1024),
        cost_estimate=pl.CostEstimate(
            flops=2 * classes * tile * width * (leaf_rows + width), bytes_accessed=2 * kernels.size,
            transcendentals=0,
        ),
    )(slot, rows_all, kernels, coarse_slot, coarse_rows, transfer)


def on_device(
    multipoles,
    kernels,
    transfer,
    leaf_target,
    leaf_source,
    leaf_count,
    coarse_target,
    coarse_source,
    coarse_count,
    ghost_send,
    coarse_send,
):
    width = multipoles.shape[1]
    rounds = lax.axis_size("leaf").bit_length() - 1
    boxes = multipoles.shape[0]
    parents = boxes // 8
    classes = kernels.shape[0]
    leaf_ghost = ghost_send.shape[2]
    coarse_ghost = coarse_send.shape[2]
    leaf_rows = boxes + rounds * leaf_ghost
    coarse_rows = parents + rounds * coarse_ghost

    child = 8 * lax.broadcasted_iota(jnp.int32, (16, parents), 1) + lax.broadcasted_iota(
        jnp.int32, (16, parents), 0
    )
    child = jnp.where(child % 8 == lax.broadcasted_iota(jnp.int32, (16, parents), 0), child, boxes)

    coarse_slot = slot_table(coarse_target[0], coarse_source[0], coarse_count[0], coarse_rows)
    chunks = 4
    devices = lax.axis_size("off")
    span = parents // devices
    per = 8 // chunks
    coarse_slot = jnp.pad(coarse_slot, ((0, 16 - classes), (0, 0)), constant_values=coarse_rows)

    leaf_region = -(-leaf_rows // coarse_rows) * coarse_rows
    rows_all = jnp.zeros((leaf_region + coarse_rows, width), multipoles.dtype)
    rows_all = lax.dynamic_update_slice(rows_all, multipoles, (0, 0))
    parent = translate(child, rows_all, transfer, 0, parents, rows=boxes).astype(jnp.bfloat16)
    rows_all = lax.dynamic_update_slice(rows_all, parent, (leaf_region, 0))
    group = -(-classes // (rounds - 1))
    groups = [(low, min(low + group, classes)) for low in range(0, classes, group)]
    slot_parts = []
    for bit_index in range(rounds):
        picks = jnp.concatenate([ghost_send[0, bit_index], coarse_send[0, bit_index] + leaf_region])
        outgoing = rows_all[picks]
        if bit_index < len(groups):
            low, high = groups[bit_index]
            tables, outgoing = lax.optimization_barrier(
                ((leaf_target[0, low:high], leaf_source[0, low:high], leaf_count[0, low:high]), outgoing)
            )
        arrived = partner(outgoing, "leaf", bit_index)
        if bit_index < len(groups):
            part, arrived = lax.optimization_barrier((slot_table(*tables, leaf_rows), arrived))
            slot_parts.append(part)
        rows_all = lax.dynamic_update_slice(
            rows_all, arrived[:leaf_ghost], (boxes + bit_index * leaf_ghost, 0)
        )
        rows_all = lax.dynamic_update_slice(
            rows_all, arrived[leaf_ghost:], (leaf_region + parents + bit_index * coarse_ghost, 0)
        )

    leaf_slot = jnp.concatenate(slot_parts, axis=0)
    leaf_slot = leaf_slot.reshape(classes, devices, span, chunks, per)
    leaf_slot = leaf_slot.transpose(0, 3, 1, 4, 2).reshape(classes, boxes)
    leaf_slot = jnp.pad(leaf_slot, ((0, 16 - classes), (0, 0)), constant_values=leaf_rows)
    tile = boxes // chunks
    block = tile // devices
    me = lax.axis_index("off")
    mine = []
    for chunk in range(chunks):
        slot_in = leaf_slot
        if chunk >= 2:
            slot_in, _ = lax.optimization_barrier((leaf_slot, mine[chunk - 2]))
        if chunk == 0:
            partial_sum, coarse_high, coarse_low = first_chunk(
                slot_in, rows_all, leaf_rows, kernels, coarse_slot, rows_all[leaf_region:],
                transfer, tile, devices,
            )
        else:
            partial_sum = translate(
                slot_in, rows_all, kernels, chunk, tile, (coarse_high, coarse_low, transfer),
                devices, rows=leaf_rows,
            )
        total = lax.dynamic_slice_in_dim(partial_sum, me * block, block, 0)
        for shift in range(1, devices):
            theirs = lax.rem(me + shift, devices)
            sent = lax.dynamic_slice_in_dim(partial_sum, theirs * block, block, 0)
            route = [(k, (k + shift) % devices) for k in range(devices)]
            total = total + lax.ppermute(sent, "off", route)
        mine.append(total)
    mine = jnp.stack(mine).reshape(8, span, width)
    return mine.transpose(1, 0, 2).reshape(-1, width)


def solution(mesh):
    in_specs = (
        P("leaf", None),
        P("off", None, None),
        P(),
        P("leaf", "off", None),
        P("leaf", "off", None),
        P("leaf", "off"),
        P("leaf", "off", None),
        P("leaf", "off", None),
        P("leaf", "off"),
        P("leaf", None, None),
        P("leaf", None, None),
    )
    out_specs = P(("leaf", "off"), None)
    return jax.shard_map(
        on_device, mesh=mesh, in_specs=in_specs, out_specs=out_specs, check_vma=False
    )
```

```python
import functools

import jax
import jax.numpy as jnp
from jax import lax
from jax.experimental import pallas as pl
from jax.experimental.pallas import tpu as pltpu
from jax.sharding import PartitionSpec as P


def partner(block, axis, apart):
    count = lax.axis_size(axis)
    route = []
    for low in range(count):
        high = low | 1 << apart
        if high != low and high < count:
            route += [(low, high), (high, low)]
    return lax.ppermute(block, axis, route)


def invert_kernel(target_ref, payload_ref, out_ref):
    pairs = target_ref.shape[1]
    columns = jnp.transpose(target_ref[...])
    spots = lax.broadcasted_iota(jnp.int32, (pairs, pairs), 1)
    for c in range(payload_ref.shape[0]):
        hot = (columns[:, c:c + 1] == spots).astype(payload_ref.dtype)
        parts = jnp.dot(payload_ref[c], hot, preferred_element_type=jnp.float32)
        out_ref[c:c + 1, :] = (parts[0:1] * 64.0 + parts[1:2]).astype(jnp.int32)


def slot_table(target, source, pair_count, pad_row):
    classes, pairs = target.shape
    pair = lax.broadcasted_iota(jnp.int32, target.shape, 1)
    payload = jnp.where(pair < pair_count[:, None], source, pad_row)
    split = jnp.stack([payload // 64, payload % 64], axis=1).astype(jnp.bfloat16)
    split = jnp.pad(split, ((0, 0), (0, 6), (0, 0)))
    target = jnp.pad(target, ((0, 16 - classes), (0, 0)), constant_values=-1)
    return pl.pallas_call(
        invert_kernel,
        out_shape=jax.ShapeDtypeStruct((classes, pairs), jnp.int32),
        compiler_params=pltpu.CompilerParams(vmem_limit_bytes=48 * 1024 * 1024),
        cost_estimate=pl.CostEstimate(
            flops=2 * 8 * classes * pairs * pairs, bytes_accessed=24 * classes * pairs, transcendentals=0
        ),
    )(target, split)


def translate_kernel(spread, devices, classes, slot_ref, buf_ref, k_ref, *rest):
    *rest, column_ref = rest
    step = pl.program_id(0)
    out_ref = rest[-1]

    def init(rest):
        if spread:
            high_ref, low_ref, t_ref, out_ref = rest
            nt = (((1,), (1,)), ((), ()))
            octants = t_ref.shape[0]
            span = high_ref.shape[0] // devices
            for h in range(octants):
                term = lax.dot_general(
                    high_ref[...], t_ref[h], nt, preferred_element_type=jnp.float32
                ) + lax.dot_general(low_ref[...], t_ref[h], nt, preferred_element_type=jnp.float32)
                for d in range(devices):
                    at = (d * octants + h) * span
                    out_ref[at:at + span, :] = term[d * span:(d + 1) * span]
        else:
            (out_ref,) = rest
            out_ref[...] = jnp.zeros(out_ref.shape, out_ref.dtype)

    @pl.when(step == 0)
    def _():
        init(rest)
        columns = jnp.transpose(slot_ref[...])
        for c in range(classes):
            column_ref[c] = columns[:, c:c + 1]

    rows = buf_ref.shape[0]
    tile = out_ref.shape[0]
    per_step = k_ref.shape[0]

    def one_class(c, carry):
        spots = lax.broadcasted_iota(jnp.int32, (tile, rows), 1)
        hot = (column_ref[step * per_step + c] == spots).astype(buf_ref.dtype)
        picked = jnp.dot(hot, buf_ref[...], preferred_element_type=jnp.float32)
        out_ref[...] += jnp.dot(
            picked.astype(k_ref.dtype), k_ref[c], preferred_element_type=jnp.float32
        )
        return carry

    lax.fori_loop(0, per_step, one_class, 0, unroll=True)


def translate(slot, buffer, kernels, chunk, tile, spread=None, devices=1, rows=None, row_block=0):
    classes = kernels.shape[0]
    width = buffer.shape[1]
    rows = rows or buffer.shape[0]
    in_specs = [
        pl.BlockSpec((slot.shape[0], tile), lambda g: (0, chunk)),
        pl.BlockSpec((rows, width), lambda g: (row_block, 0)),
        pl.BlockSpec((classes // 2, width, width), lambda g: (g, 0, 0)),
    ]
    operands = [slot, buffer, kernels]
    if spread is not None:
        high, low, transfer = spread
        octants = tile // high.shape[0]
        in_specs += [
            pl.BlockSpec(high.shape, lambda g: (0, 0)),
            pl.BlockSpec(low.shape, lambda g: (0, 0)),
            pl.BlockSpec((octants, width, width), lambda g: (chunk, 0, 0)),
        ]
        operands += [high, low, transfer]
    flops = 2 * classes * tile * width * (rows + width)
    return pl.pallas_call(
        functools.partial(translate_kernel, spread is not None, devices, classes),
        grid=(2,),
        in_specs=in_specs,
        out_specs=pl.BlockSpec((tile, width), lambda g: (0, 0)),
        out_shape=jax.ShapeDtypeStruct((tile, width), jnp.float32),
        scratch_shapes=[pltpu.VMEM((slot.shape[0], tile, 1), jnp.int32)],
        compiler_params=pltpu.CompilerParams(vmem_limit_bytes=48 * 1024 * 1024),
        cost_estimate=pl.CostEstimate(
            flops=flops, bytes_accessed=2 * kernels.size + 2 * buffer.size, transcendentals=0
        ),
    )(*operands)


def first_kernel(devices, classes, slot_ref, buf_ref, k_ref, cslot_ref, cbuf_ref, t_ref,
                 out_ref, high_ref, low_ref, column_ref, ccolumn_ref, cacc_ref):
    step = pl.program_id(0)
    per_step = k_ref.shape[0]

    @pl.when(step == 0)
    def _():
        out_ref[...] = jnp.zeros(out_ref.shape, out_ref.dtype)
        cacc_ref[...] = jnp.zeros(cacc_ref.shape, cacc_ref.dtype)
        columns = jnp.transpose(slot_ref[...])
        ccolumns = jnp.transpose(cslot_ref[...])
        for c in range(classes):
            column_ref[c] = columns[:, c:c + 1]
            ccolumn_ref[c] = ccolumns[:, c:c + 1]

    def one_class(c, carry):
        k = k_ref[c]
        spots = lax.broadcasted_iota(jnp.int32, (out_ref.shape[0], buf_ref.shape[0]), 1)
        hot = (column_ref[step * per_step + c] == spots).astype(buf_ref.dtype)
        picked = jnp.dot(hot, buf_ref[...], preferred_element_type=jnp.float32)
        out_ref[...] += jnp.dot(picked.astype(k.dtype), k, preferred_element_type=jnp.float32)
        cspots = lax.broadcasted_iota(jnp.int32, (cacc_ref.shape[0], cbuf_ref.shape[0]), 1)
        chot = (ccolumn_ref[step * per_step + c] == cspots).astype(cbuf_ref.dtype)
        cpicked = jnp.dot(chot, cbuf_ref[...], preferred_element_type=jnp.float32)
        cacc_ref[...] += jnp.dot(cpicked.astype(k.dtype), k, preferred_element_type=jnp.float32)
        return carry

    lax.fori_loop(0, per_step, one_class, 0, unroll=True)

    @pl.when(step == pl.num_programs(0) - 1)
    def _():
        local = 0.5 * cacc_ref[...]
        high = local.astype(high_ref.dtype)
        low = (local - high.astype(jnp.float32)).astype(low_ref.dtype)
        high_ref[...] = high
        low_ref[...] = low
        nt = (((1,), (1,)), ((), ()))
        octants = t_ref.shape[0]
        span = high.shape[0] // devices
        for h in range(octants):
            term = lax.dot_general(
                high, t_ref[h], nt, preferred_element_type=jnp.float32
            ) + lax.dot_general(low, t_ref[h], nt, preferred_element_type=jnp.float32)
            for d in range(devices):
                at = (d * octants + h) * span
                out_ref[at:at + span, :] += term[d * span:(d + 1) * span]


def first_chunk(slot, rows_all, leaf_rows, kernels, coarse_slot, coarse_rows, transfer, tile, devices):
    classes = kernels.shape[0]
    width = rows_all.shape[1]
    parents = coarse_slot.shape[1]
    octants = tile // parents
    return pl.pallas_call(
        functools.partial(first_kernel, devices, classes),
        grid=(2,),
        in_specs=[
            pl.BlockSpec((slot.shape[0], tile), lambda g: (0, 0)),
            pl.BlockSpec((leaf_rows, width), lambda g: (0, 0)),
            pl.BlockSpec((classes // 2, width, width), lambda g: (g, 0, 0)),
            pl.BlockSpec(coarse_slot.shape, lambda g: (0, 0)),
            pl.BlockSpec(coarse_rows.shape, lambda g: (0, 0)),
            pl.BlockSpec((octants, width, width), lambda g: (0, 0, 0)),
        ],
        out_specs=[
            pl.BlockSpec((tile, width), lambda g: (0, 0)),
            pl.BlockSpec((parents, width), lambda g: (0, 0)),
            pl.BlockSpec((parents, width), lambda g: (0, 0)),
        ],
        out_shape=[
            jax.ShapeDtypeStruct((tile, width), jnp.float32),
            jax.ShapeDtypeStruct((parents, width), jnp.bfloat16),
            jax.ShapeDtypeStruct((parents, width), jnp.bfloat16),
        ],
        scratch_shapes=[
            pltpu.VMEM((slot.shape[0], tile, 1), jnp.int32),
            pltpu.VMEM((coarse_slot.shape[0], parents, 1), jnp.int32),
            pltpu.VMEM((parents, width), jnp.float32),
        ],
        compiler_params=pltpu.CompilerParams(vmem_limit_bytes=48 * 1024 * 1024),
        cost_estimate=pl.CostEstimate(
            flops=2 * classes * tile * width * (leaf_rows + width), bytes_accessed=2 * kernels.size,
            transcendentals=0,
        ),
    )(slot, rows_all, kernels, coarse_slot, coarse_rows, transfer)


def on_device(
    multipoles,
    kernels,
    transfer,
    leaf_target,
    leaf_source,
    leaf_count,
    coarse_target,
    coarse_source,
    coarse_count,
    ghost_send,
    coarse_send,
):
    width = multipoles.shape[1]
    rounds = lax.axis_size("leaf").bit_length() - 1
    boxes = multipoles.shape[0]
    parents = boxes // 8
    classes = kernels.shape[0]
    leaf_ghost = ghost_send.shape[2]
    coarse_ghost = coarse_send.shape[2]
    leaf_rows = boxes + rounds * leaf_ghost
    coarse_rows = parents + rounds * coarse_ghost

    child = 8 * lax.broadcasted_iota(jnp.int32, (16, parents), 1) + lax.broadcasted_iota(
        jnp.int32, (16, parents), 0
    )
    child = jnp.where(child % 8 == lax.broadcasted_iota(jnp.int32, (16, parents), 0), child, boxes)

    coarse_slot = slot_table(coarse_target[0], coarse_source[0], coarse_count[0], coarse_rows)
    chunks = 4
    devices = lax.axis_size("off")
    span = parents // devices
    per = 8 // chunks
    coarse_slot = jnp.pad(coarse_slot, ((0, 16 - classes), (0, 0)), constant_values=coarse_rows)

    leaf_region = -(-leaf_rows // coarse_rows) * coarse_rows
    rows_all = jnp.zeros((leaf_region + coarse_rows, width), multipoles.dtype)
    rows_all = lax.dynamic_update_slice(rows_all, multipoles, (0, 0))
    parent = translate(child, rows_all, transfer, 0, parents, rows=boxes).astype(jnp.bfloat16)
    rows_all = lax.dynamic_update_slice(rows_all, parent, (leaf_region, 0))
    group = -(-classes // (rounds - 1))
    groups = [(low, min(low + group, classes)) for low in range(0, classes, group)]
    slot_parts = []
    for bit_index in range(rounds):
        picks = jnp.concatenate([ghost_send[0, bit_index], coarse_send[0, bit_index] + leaf_region])
        outgoing = rows_all[picks]
        if bit_index < len(groups):
            low, high = groups[bit_index]
            tables, outgoing = lax.optimization_barrier(
                ((leaf_target[0, low:high], leaf_source[0, low:high], leaf_count[0, low:high]), outgoing)
            )
        arrived = partner(outgoing, "leaf", bit_index)
        if bit_index < len(groups):
            part, arrived = lax.optimization_barrier((slot_table(*tables, leaf_rows), arrived))
            slot_parts.append(part)
        rows_all = lax.dynamic_update_slice(
            rows_all, arrived[:leaf_ghost], (boxes + bit_index * leaf_ghost, 0)
        )
        rows_all = lax.dynamic_update_slice(
            rows_all, arrived[leaf_ghost:], (leaf_region + parents + bit_index * coarse_ghost, 0)
        )

    leaf_slot = jnp.concatenate(slot_parts, axis=0)
    leaf_slot = leaf_slot.reshape(classes, devices, span, chunks, per)
    leaf_slot = leaf_slot.transpose(0, 3, 1, 4, 2).reshape(classes, boxes)
    leaf_slot = jnp.pad(leaf_slot, ((0, 16 - classes), (0, 0)), constant_values=leaf_rows)
    tile = boxes // chunks
    block = tile // devices
    me = lax.axis_index("off")
    mine = []
    for chunk in range(chunks):
        slot_in = leaf_slot
        if chunk >= 2:
            slot_in, _ = lax.optimization_barrier((leaf_slot, mine[chunk - 2]))
        if chunk == 0:
            partial_sum, coarse_high, coarse_low = first_chunk(
                slot_in, rows_all, leaf_rows, kernels, coarse_slot, rows_all[leaf_region:],
                transfer, tile, devices,
            )
        else:
            partial_sum = translate(
                slot_in, rows_all, kernels, chunk, tile, (coarse_high, coarse_low, transfer),
                devices, rows=leaf_rows,
            )
        total = lax.dynamic_slice_in_dim(partial_sum, me * block, block, 0)
        for shift in range(1, devices):
            theirs = lax.rem(me + shift, devices)
            sent = lax.dynamic_slice_in_dim(partial_sum, theirs * block, block, 0)
            route = [(k, (k + shift) % devices) for k in range(devices)]
            total = total + lax.ppermute(sent, "off", route)
        mine.append(total)
    result = jnp.zeros((span, 8, width), jnp.float32)
    for chunk, total in enumerate(mine):
        placed = total.reshape(per, span, width).transpose(1, 0, 2)
        result = lax.dynamic_update_slice(result, placed, (0, chunk * per, 0))
    return result.reshape(-1, width)


def solution(mesh):
    in_specs = (
        P("leaf", None),
        P("off", None, None),
        P(),
        P("leaf", "off", None),
        P("leaf", "off", None),
        P("leaf", "off"),
        P("leaf", "off", None),
        P("leaf", "off", None),
        P("leaf", "off"),
        P("leaf", None, None),
        P("leaf", None, None),
    )
    out_specs = P(("leaf", "off"), None)
    return jax.shard_map(
        on_device, mesh=mesh, in_specs=in_specs, out_specs=out_specs, check_vma=False
    )
```

```python
import functools

import jax
import jax.numpy as jnp
from jax import lax
from jax.experimental import pallas as pl
from jax.experimental.pallas import tpu as pltpu
from jax.sharding import PartitionSpec as P


def partner(block, axis, apart):
    count = lax.axis_size(axis)
    route = []
    for low in range(count):
        high = low | 1 << apart
        if high != low and high < count:
            route += [(low, high), (high, low)]
    return lax.ppermute(block, axis, route)


def invert_kernel(target_ref, payload_ref, out_ref):
    pairs = target_ref.shape[1]
    columns = jnp.transpose(target_ref[...])
    spots = lax.broadcasted_iota(jnp.int32, (pairs, pairs), 1)
    for c in range(payload_ref.shape[0]):
        hot = (columns[:, c:c + 1] == spots).astype(payload_ref.dtype)
        parts = jnp.dot(payload_ref[c], hot, preferred_element_type=jnp.float32)
        out_ref[c:c + 1, :] = (parts[0:1] * 64.0 + parts[1:2]).astype(jnp.int32)


def slot_table(target, source, pair_count, pad_row):
    classes, pairs = target.shape
    pair = lax.broadcasted_iota(jnp.int32, target.shape, 1)
    payload = jnp.where(pair < pair_count[:, None], source, pad_row)
    split = jnp.stack([payload // 64, payload % 64], axis=1).astype(jnp.bfloat16)
    split = jnp.pad(split, ((0, 0), (0, 6), (0, 0)))
    target = jnp.pad(target, ((0, 16 - classes), (0, 0)), constant_values=-1)
    return pl.pallas_call(
        invert_kernel,
        out_shape=jax.ShapeDtypeStruct((classes, pairs), jnp.int32),
        compiler_params=pltpu.CompilerParams(vmem_limit_bytes=48 * 1024 * 1024),
        cost_estimate=pl.CostEstimate(
            flops=2 * 8 * classes * pairs * pairs, bytes_accessed=24 * classes * pairs, transcendentals=0
        ),
    )(target, split)


def translate_kernel(spread, devices, classes, slot_ref, buf_ref, k_ref, *rest):
    *rest, column_ref = rest
    step = pl.program_id(0)
    out_ref = rest[-1]

    def init(rest):
        if spread:
            high_ref, low_ref, t_ref, out_ref = rest
            nt = (((1,), (1,)), ((), ()))
            octants = t_ref.shape[0]
            span = high_ref.shape[0] // devices
            for h in range(octants):
                term = lax.dot_general(
                    high_ref[...], t_ref[h], nt, preferred_element_type=jnp.float32
                ) + lax.dot_general(low_ref[...], t_ref[h], nt, preferred_element_type=jnp.float32)
                for d in range(devices):
                    at = (d * octants + h) * span
                    out_ref[at:at + span, :] = term[d * span:(d + 1) * span]
        else:
            (out_ref,) = rest
            out_ref[...] = jnp.zeros(out_ref.shape, out_ref.dtype)

    @pl.when(step == 0)
    def _():
        init(rest)
        columns = jnp.transpose(slot_ref[...])
        for c in range(classes):
            column_ref[c] = columns[:, c:c + 1]

    rows = buf_ref.shape[0]
    tile = out_ref.shape[0]
    per_step = k_ref.shape[0]

    def one_class(c, carry):
        spots = lax.broadcasted_iota(jnp.int32, (tile, rows), 1)
        hot = (column_ref[step * per_step + c] == spots).astype(buf_ref.dtype)
        picked = jnp.dot(hot, buf_ref[...], preferred_element_type=jnp.float32)
        out_ref[...] += jnp.dot(
            picked.astype(k_ref.dtype), k_ref[c], preferred_element_type=jnp.float32
        )
        return carry

    lax.fori_loop(0, per_step, one_class, 0, unroll=True)


def translate(slot, buffer, kernels, chunk, tile, spread=None, devices=1, rows=None, row_block=0):
    classes = kernels.shape[0]
    width = buffer.shape[1]
    rows = rows or buffer.shape[0]
    in_specs = [
        pl.BlockSpec((slot.shape[0], tile), lambda g: (0, chunk)),
        pl.BlockSpec((rows, width), lambda g: (row_block, 0)),
        pl.BlockSpec((classes // 2, width, width), lambda g: (g, 0, 0)),
    ]
    operands = [slot, buffer, kernels]
    if spread is not None:
        high, low, transfer = spread
        octants = tile // high.shape[0]
        in_specs += [
            pl.BlockSpec(high.shape, lambda g: (0, 0)),
            pl.BlockSpec(low.shape, lambda g: (0, 0)),
            pl.BlockSpec((octants, width, width), lambda g: (chunk, 0, 0)),
        ]
        operands += [high, low, transfer]
    flops = 2 * classes * tile * width * (rows + width)
    return pl.pallas_call(
        functools.partial(translate_kernel, spread is not None, devices, classes),
        grid=(2,),
        in_specs=in_specs,
        out_specs=pl.BlockSpec((tile, width), lambda g: (0, 0)),
        out_shape=jax.ShapeDtypeStruct((tile, width), jnp.float32),
        scratch_shapes=[pltpu.VMEM((slot.shape[0], tile, 1), jnp.int32)],
        compiler_params=pltpu.CompilerParams(vmem_limit_bytes=48 * 1024 * 1024),
        cost_estimate=pl.CostEstimate(
            flops=flops, bytes_accessed=2 * kernels.size + 2 * buffer.size, transcendentals=0
        ),
    )(*operands)


def first_kernel(devices, classes, slot_ref, buf_ref, k_ref, cslot_ref, cbuf_ref, t_ref,
                 out_ref, high_ref, low_ref, column_ref, ccolumn_ref, cacc_ref):
    step = pl.program_id(0)
    per_step = k_ref.shape[0]

    @pl.when(step == 0)
    def _():
        out_ref[...] = jnp.zeros(out_ref.shape, out_ref.dtype)
        cacc_ref[...] = jnp.zeros(cacc_ref.shape, cacc_ref.dtype)
        columns = jnp.transpose(slot_ref[...])
        ccolumns = jnp.transpose(cslot_ref[...])
        for c in range(classes):
            column_ref[c] = columns[:, c:c + 1]
            ccolumn_ref[c] = ccolumns[:, c:c + 1]

    def one_class(c, carry):
        k = k_ref[c]
        spots = lax.broadcasted_iota(jnp.int32, (out_ref.shape[0], buf_ref.shape[0]), 1)
        hot = (column_ref[step * per_step + c] == spots).astype(buf_ref.dtype)
        picked = jnp.dot(hot, buf_ref[...], preferred_element_type=jnp.float32)
        out_ref[...] += jnp.dot(picked.astype(k.dtype), k, preferred_element_type=jnp.float32)
        cspots = lax.broadcasted_iota(jnp.int32, (cacc_ref.shape[0], cbuf_ref.shape[0]), 1)
        chot = (ccolumn_ref[step * per_step + c] == cspots).astype(cbuf_ref.dtype)
        cpicked = jnp.dot(chot, cbuf_ref[...], preferred_element_type=jnp.float32)
        cacc_ref[...] += jnp.dot(cpicked.astype(k.dtype), k, preferred_element_type=jnp.float32)
        return carry

    lax.fori_loop(0, per_step, one_class, 0, unroll=True)

    @pl.when(step == pl.num_programs(0) - 1)
    def _():
        local = 0.5 * cacc_ref[...]
        high = local.astype(high_ref.dtype)
        low = (local - high.astype(jnp.float32)).astype(low_ref.dtype)
        high_ref[...] = high
        low_ref[...] = low
        nt = (((1,), (1,)), ((), ()))
        octants = t_ref.shape[0]
        span = high.shape[0] // devices
        for h in range(octants):
            term = lax.dot_general(
                high, t_ref[h], nt, preferred_element_type=jnp.float32
            ) + lax.dot_general(low, t_ref[h], nt, preferred_element_type=jnp.float32)
            for d in range(devices):
                at = (d * octants + h) * span
                out_ref[at:at + span, :] += term[d * span:(d + 1) * span]


def first_chunk(slot, rows_all, leaf_rows, kernels, coarse_slot, coarse_rows, transfer, tile, devices):
    classes = kernels.shape[0]
    width = rows_all.shape[1]
    parents = coarse_slot.shape[1]
    octants = tile // parents
    return pl.pallas_call(
        functools.partial(first_kernel, devices, classes),
        grid=(2,),
        in_specs=[
            pl.BlockSpec((slot.shape[0], tile), lambda g: (0, 0)),
            pl.BlockSpec((leaf_rows, width), lambda g: (0, 0)),
            pl.BlockSpec((classes // 2, width, width), lambda g: (g, 0, 0)),
            pl.BlockSpec(coarse_slot.shape, lambda g: (0, 0)),
            pl.BlockSpec(coarse_rows.shape, lambda g: (0, 0)),
            pl.BlockSpec((octants, width, width), lambda g: (0, 0, 0)),
        ],
        out_specs=[
            pl.BlockSpec((tile, width), lambda g: (0, 0)),
            pl.BlockSpec((parents, width), lambda g: (0, 0)),
            pl.BlockSpec((parents, width), lambda g: (0, 0)),
        ],
        out_shape=[
            jax.ShapeDtypeStruct((tile, width), jnp.float32),
            jax.ShapeDtypeStruct((parents, width), jnp.bfloat16),
            jax.ShapeDtypeStruct((parents, width), jnp.bfloat16),
        ],
        scratch_shapes=[
            pltpu.VMEM((slot.shape[0], tile, 1), jnp.int32),
            pltpu.VMEM((coarse_slot.shape[0], parents, 1), jnp.int32),
            pltpu.VMEM((parents, width), jnp.float32),
        ],
        compiler_params=pltpu.CompilerParams(vmem_limit_bytes=48 * 1024 * 1024),
        cost_estimate=pl.CostEstimate(
            flops=2 * classes * tile * width * (leaf_rows + width), bytes_accessed=2 * kernels.size,
            transcendentals=0,
        ),
    )(slot, rows_all, kernels, coarse_slot, coarse_rows, transfer)


def on_device(
    multipoles,
    kernels,
    transfer,
    leaf_target,
    leaf_source,
    leaf_count,
    coarse_target,
    coarse_source,
    coarse_count,
    ghost_send,
    coarse_send,
):
    width = multipoles.shape[1]
    rounds = lax.axis_size("leaf").bit_length() - 1
    boxes = multipoles.shape[0]
    parents = boxes // 8
    classes = kernels.shape[0]
    leaf_ghost = ghost_send.shape[2]
    coarse_ghost = coarse_send.shape[2]
    leaf_rows = boxes + rounds * leaf_ghost
    coarse_rows = parents + rounds * coarse_ghost

    child = 8 * lax.broadcasted_iota(jnp.int32, (16, parents), 1) + lax.broadcasted_iota(
        jnp.int32, (16, parents), 0
    )
    child = jnp.where(child % 8 == lax.broadcasted_iota(jnp.int32, (16, parents), 0), child, boxes)

    coarse_slot = slot_table(coarse_target[0], coarse_source[0], coarse_count[0], coarse_rows)
    chunks = 4
    devices = lax.axis_size("off")
    span = parents // devices
    per = 8 // chunks
    coarse_slot = jnp.pad(coarse_slot, ((0, 16 - classes), (0, 0)), constant_values=coarse_rows)

    leaf_region = -(-leaf_rows // coarse_rows) * coarse_rows
    rows_all = jnp.zeros((leaf_region + coarse_rows, width), multipoles.dtype)
    rows_all = lax.dynamic_update_slice(rows_all, multipoles, (0, 0))
    parent = translate(child, rows_all, transfer, 0, parents, rows=boxes).astype(jnp.bfloat16)
    rows_all = lax.dynamic_update_slice(rows_all, parent, (leaf_region, 0))
    group = -(-classes // (rounds - 1))
    groups = [(low, min(low + group, classes)) for low in range(0, classes, group)]
    slot_parts = []
    for bit_index in range(rounds):
        picks = jnp.concatenate([ghost_send[0, bit_index], coarse_send[0, bit_index] + leaf_region])
        outgoing = rows_all[picks]
        if bit_index < len(groups):
            low, high = groups[bit_index]
            tables, outgoing = lax.optimization_barrier(
                ((leaf_target[0, low:high], leaf_source[0, low:high], leaf_count[0, low:high]), outgoing)
            )
        arrived = partner(outgoing, "leaf", bit_index)
        if bit_index < len(groups):
            part, arrived = lax.optimization_barrier((slot_table(*tables, leaf_rows), arrived))
            slot_parts.append(part)
        rows_all = lax.dynamic_update_slice(
            rows_all, arrived[:leaf_ghost], (boxes + bit_index * leaf_ghost, 0)
        )
        rows_all = lax.dynamic_update_slice(
            rows_all, arrived[leaf_ghost:], (leaf_region + parents + bit_index * coarse_ghost, 0)
        )

    leaf_slot = jnp.concatenate(slot_parts, axis=0)
    leaf_slot = leaf_slot.reshape(classes, devices, span, chunks, per)
    leaf_slot = leaf_slot.transpose(0, 3, 1, 4, 2).reshape(classes, boxes)
    leaf_slot = jnp.pad(leaf_slot, ((0, 16 - classes), (0, 0)), constant_values=leaf_rows)
    tile = boxes // chunks
    block = tile // devices
    me = lax.axis_index("off")
    mine = []
    for chunk in range(chunks):
        slot_in = leaf_slot
        if chunk >= 3:
            slot_in, _ = lax.optimization_barrier((leaf_slot, mine[chunk - 3]))
        if chunk == 0:
            partial_sum, coarse_high, coarse_low = first_chunk(
                slot_in, rows_all, leaf_rows, kernels, coarse_slot, rows_all[leaf_region:],
                transfer, tile, devices,
            )
        else:
            partial_sum = translate(
                slot_in, rows_all, kernels, chunk, tile, (coarse_high, coarse_low, transfer),
                devices, rows=leaf_rows,
            )
        total = lax.dynamic_slice_in_dim(partial_sum, me * block, block, 0)
        for shift in range(1, devices):
            theirs = lax.rem(me + shift, devices)
            sent = lax.dynamic_slice_in_dim(partial_sum, theirs * block, block, 0)
            route = [(k, (k + shift) % devices) for k in range(devices)]
            total = total + lax.ppermute(sent, "off", route)
        mine.append(total)
    mine = jnp.stack(mine).reshape(8, span, width)
    return mine.transpose(1, 0, 2).reshape(-1, width)


def solution(mesh):
    in_specs = (
        P("leaf", None),
        P("off", None, None),
        P(),
        P("leaf", "off", None),
        P("leaf", "off", None),
        P("leaf", "off"),
        P("leaf", "off", None),
        P("leaf", "off", None),
        P("leaf", "off"),
        P("leaf", None, None),
        P("leaf", None, None),
    )
    out_specs = P(("leaf", "off"), None)
    return jax.shard_map(
        on_device, mesh=mesh, in_specs=in_specs, out_specs=out_specs, check_vma=False
    )
```
